32 devices in a mesh: shots: 2 (over y), depth: 4 (over x, core), freq: 4 (over z).
Axes of the slice: x: 2, y: 2, z: 4, core: 2. Of those that a mesh axis runs over, the one named last changes fastest.
Arguments:
- surface: bfloat16 [4, 4, 2, 384, 384], P('shots', 'freq'), parts along dimension 0, may hold values from -6 to 6
- kernels: bfloat16 [4, 4, 2, 25, 25], P('depth', 'freq'), may hold values from -0.15625 to 0.15625
- slowness: float32 [4, 384, 384], P('depth'), may hold values from -0.02 to 0.02
- freq_index: int32 [4], P('freq'), may hold values from 8 to 199
Outputs:
- image: float32 [8, 384, 384], P(('shots', 'depth'), 'freq'), parts along dimension 0
The draws below stay inside these ranges and needn't reach their ends.
There are 2 independent parts, one for each index of `shots`. The reference program is written for one: setup_inputs(seed, part) draws one part's arguments, and reference() takes and returns one part's arrays. A program takes and returns all parts, laid end to end along the dimension named above; an argument that names none is the same for every part. Nothing has to cross between parts.
All inputs are finite; a program needn't handle non-finite values.
Results may differ from the reference program's by a relative error of at most 0.0067.
Values may be sent and summed in bfloat16 or wider, within the bound.
A program may use at most 64 MiB of HBM per device.

```python
import math
import jax
import jax.numpy as jnp
from jax import lax

LX = 384
LY = 384
KW = 25
NF = 4
NZ = 4


def touch_ends(entries, rng, low, largest):
    spot = [jax.random.randint(jax.random.fold_in(rng, axis), (), 0, length) for axis, length in enumerate(entries.shape)]
    longest = entries.shape.index(max(entries.shape))
    beside = spot[:longest] + [(spot[longest] + 1) % entries.shape[longest]] + spot[longest + 1:]
    return entries.at[tuple(spot)].set(low).at[tuple(beside)].set(largest)


def steps_of(key, dims, shards, low, top_value):
    def one(position, parts):
        heights = jax.random.uniform(jax.random.fold_in(jax.random.fold_in(key, 6), position), (parts,), jnp.float32, low / len(shards), top_value / len(shards))
        return jnp.repeat(jnp.exp(heights), dims[position] // parts).reshape((-1,) + (1,) * (len(dims) - position - 1))

    factor_of = one(*shards[0])
    for cut in shards[1:]:
        factor_of = factor_of * one(*cut)
    return factor_of


def gaussian(own_key, shape, deviation, reach, shards=(), dtype=jnp.bfloat16):
    array = deviation * jax.random.normal(own_key, shape, jnp.float32)
    if shards:
        array = array * steps_of(own_key, shape, shards, -0.22, 0.18)
    return jnp.clip(array, -reach, reach).astype(dtype)


def setup_inputs(seed: int = 0, part: int = 0) -> dict:
    keys = jax.random.split(jax.random.key(seed), 5)
    part_keys = jax.random.split(jax.random.fold_in(keys[4], part), 5)
    surface = gaussian(part_keys[0], (2, NF, 2, LX, LY), 1.0, 6.0, ((1, 4),))
    kernels = gaussian(keys[1], (NZ, NF, 2, KW, KW), (2 * KW * KW) ** -0.5, 0.15625, ((0, 4), (1, 4)))
    slowness = jnp.clip(jax.random.uniform(keys[2], (NZ, LX, LY), jnp.float32, -0.02, 0.02) * steps_of(keys[2], (NZ, LX, LY), ((0, 4),), -0.4, 0.0), -0.02, 0.02)
    freq_index = touch_ends(jax.random.randint(keys[3], (NF,), 8, 200), jax.random.fold_in(keys[3], 1), 8, 199).astype(jnp.int32)
    return {"surface": surface, "kernels": kernels, "slowness": slowness, "freq_index": freq_index}


def extrapolate(wavefield, stencil, phase_rate, freq_bins):
    freq_count = wavefield.shape[1]
    cells_x = wavefield.shape[3]
    cells_y = wavefield.shape[4]
    tap_count = stencil.shape[-1]
    stacked = wavefield.reshape(2, freq_count * 2, cells_x, cells_y)
    real_part = stencil[:, 0]
    imag_part = stencil[:, 1]
    filters = jnp.stack([jnp.stack([real_part, -imag_part], 1), jnp.stack([imag_part, real_part], 1)], 1)
    filters = filters.reshape(freq_count * 2, 2, tap_count, tap_count)
    convolved = lax.conv_general_dilated(stacked, filters, (1, 1), 'SAME', dimension_numbers=('NCHW', 'OIHW', 'NCHW'), feature_group_count=freq_count, preferred_element_type=jnp.float32)
    convolved = convolved.reshape(2, freq_count, 2, cells_x, cells_y)
    phases = freq_bins.astype(jnp.float32)[:, None, None] * phase_rate[None]
    cosines = jnp.cos(phases)
    sine_terms = jnp.sin(phases)
    real_out = convolved[:, :, 0] * cosines - convolved[:, :, 1] * sine_terms
    imag_out = convolved[:, :, 0] * sine_terms + convolved[:, :, 1] * cosines
    stepped = jnp.stack([real_out, imag_out], 2).astype(jnp.bfloat16)
    widened = stepped.astype(jnp.float32)
    partial_sum = lax.optimization_barrier(jnp.sum(widened[0, :, 0] * widened[1, :, 0] + widened[0, :, 1] * widened[1, :, 1], axis=0))
    return (stepped, partial_sum)

def reference(surface, kernels, slowness, freq_index):

    def advance(wavefield, operands):
        stencil, phase_rate = operands
        stepped, partial_sum = extrapolate(wavefield, stencil, phase_rate, freq_index)
        return (stepped, partial_sum)
    final_wave, partials = lax.scan(advance, surface, (kernels, slowness))
    return partials * (1.0 / math.sqrt(NF))
```

```python
import functools
import math

import jax
import jax.numpy as jnp
from jax import lax
from jax.experimental import pallas as pl
from jax.experimental.pallas import tpu as pltpu
from jax.sharding import PartitionSpec as P


def with_halo(shard, sides, width):
    for axis, dim in sides:
        size, length = (lax.axis_size(axis), shard.shape[dim])
        up = [(i, (i + 1) % size) for i in range(size - 1)]
        down = [(j, i) for i, j in up]
        last = lax.slice_in_dim(shard, length - width, length, axis=dim)
        leading = lax.slice_in_dim(shard, 0, width, axis=dim)
        before = lax.ppermute(last, axis, up)
        after = lax.ppermute(leading, axis, down)
        shard = jnp.concatenate([before, shard, after], axis=dim)
    return shard


def convolve(padded, stencil, margin):
    rows_in = padded.shape[3]
    cells_y = padded.shape[4]
    tap_count = stencil.shape[-1]
    rows_out = rows_in - 2 * margin
    real_part = stencil[:, 0].astype(jnp.float32)
    imag_part = stencil[:, 1].astype(jnp.float32)
    filters = jnp.stack(
        [jnp.stack([real_part, -imag_part], 1), jnp.stack([imag_part, real_part], 1)], 1
    )
    offsets = lax.iota(jnp.int32, rows_in)[None, :] - lax.iota(jnp.int32, rows_out)[:, None]
    select = (offsets[None] == lax.iota(jnp.int32, tap_count)[:, None, None]).astype(jnp.float32)
    banded = jnp.einsum("fdcab,axk->fdxbck", filters, select).astype(jnp.bfloat16)
    widened = jnp.pad(padded, ((0, 0), (0, 0), (0, 0), (0, 0), (margin, margin)))
    patches = jnp.stack(
        [widened[:, :, :, :, shift : shift + cells_y] for shift in range(tap_count)], 0
    )
    return jnp.einsum("bwfcky,fdxbck->wfdxy", patches, banded, preferred_element_type=jnp.float32)


def rotate(convolved, phase_rate, freq_bins):
    phases = freq_bins[:, None, None] * phase_rate[None]
    cosines = jnp.cos(phases)
    sine_terms = jnp.sin(phases)
    real_out = convolved[:, :, 0] * cosines - convolved[:, :, 1] * sine_terms
    imag_out = convolved[:, :, 0] * sine_terms + convolved[:, :, 1] * cosines
    return jnp.stack([real_out, imag_out], 2).astype(jnp.bfloat16)


def correlate(stepped):
    widened = stepped.astype(jnp.float32)
    return jnp.sum(
        widened[0, :, 0] * widened[1, :, 0] + widened[0, :, 1] * widened[1, :, 1], axis=0
    )


def on_device_general(surface, kernels, slowness, freq_index):
    depth_count = lax.axis_size("depth")
    position = lax.axis_index("depth")
    cells_x = surface.shape[3]
    row_count = cells_x // depth_count
    tap_count = kernels.shape[-1]
    margin = (tap_count - 1) // 2
    start_row = position * row_count
    wavefield = lax.dynamic_slice_in_dim(surface, start_row, row_count, 3)
    stencils = lax.all_gather(kernels, "depth", axis=0, tiled=True)
    phase_rates = lax.all_to_all(slowness, "depth", split_axis=1, concat_axis=0, tiled=True)
    freq_bins = freq_index.astype(jnp.float32)

    def advance(wave, operands):
        stencil, phase_rate = operands
        padded = with_halo(wave, (("depth", 3),), margin)
        stepped = rotate(convolve(padded, stencil, margin), phase_rate, freq_bins)
        return (stepped, correlate(stepped))

    final_wave, partials = lax.scan(advance, wavefield, (stencils, phase_rates))
    moved = lax.all_to_all(partials, "depth", split_axis=0, concat_axis=1, tiled=True)
    summed = lax.psum_scatter(moved, "freq", scatter_dimension=1, tiled=True)
    return summed * (1.0 / math.sqrt(surface.shape[1] * lax.axis_size("freq")))


MESH = pl.DeviceIdType.MESH
SCALE = 32767.0 / 0.02
TX, TY, REACH, STEPS, ROWS, CELLS = 8, 16, 12, 4, 96, 384
PLANE_TILES = CELLS // TX
WINDOW = (ROWS + 2 * REACH * STEPS) // TX
SINE = (1.414213201146787, -0.23570044870069473, 0.011782564917166203, -0.00027913063632810375, 3.524705887741897e-06)
COSINE = (1.4142128454174687, -0.7070977888086795, 0.0589074886457319, -0.0019514243489185956, 3.136662365288423e-05)


def iotas(rows):
    return (lax.broadcasted_iota(jnp.int32, (rows, 128), 0), lax.broadcasted_iota(jnp.int32, (rows, 128), 1))


def turn(block):
    group = iotas(8)[1] >> 4
    block = pltpu.roll(block, 16, 1, stride=16, stride_axis=0)
    for k in range(3):
        block = jnp.where((group >> k) & 1 == 1, pltpu.roll(block, 8 - (1 << k), 0), block)
    return pltpu.roll(block, 0, 1, stride=16, stride_axis=0)


def turn_back(block):
    sub, lane = iotas(8)
    group = lane >> 4
    for k in range(3):
        block = jnp.where((sub >> k) & 1 == 1, pltpu.roll(block, 128 - (16 << k), 1), block)
    for k in range(3):
        block = jnp.where((group >> k) & 1 == 1, pltpu.roll(block, 1 << k, 0), block)
    block = pltpu.roll(block, 112, 1)
    for k in range(3):
        block = jnp.where((sub >> k) & 1 == 1, pltpu.roll(block, 128 - (16 << k), 1), block)
    return block


def rotor(phase_half):
    sq = phase_half * phase_half
    sine = jnp.full_like(sq, SINE[-1])
    for value in SINE[-2::-1]:
        sine = sine * sq + value
    sine = sine * phase_half
    cosine = jnp.full_like(sq, COSINE[-1])
    for value in COSINE[-2::-1]:
        cosine = cosine * sq + value
    return sine * cosine, 1.0 - sine * sine


def emit(wave, at, values):
    plain, beside, ends = wave
    sub, lane = iotas(8)
    dy = lane & 15
    low = dy < 8
    middle = (dy >= 4) & (dy < 12)
    sides, rests = [], []
    for w in range(2):
        side, rest = [], []
        for c in range(2):
            v = values[w][c]
            down = [pltpu.roll(x, 1, 0) for x in v]
            up = [pltpu.roll(x, 7, 0) for x in v]
            after = [jnp.where(sub == 0, down[g - 1] if g else 0.0, down[g]) for g in range(3)]
            before = [jnp.where(sub == 7, up[g + 1] if g < 2 else 0.0, up[g]) for g in range(3)]
            side.append([jnp.where(low, a, b) for a, b in zip(after, before)])
            rest.append([jnp.where(low, b, a) for a, b in zip(after, before)])
        sides.append(side)
        rests.append([jnp.where(middle, a, pltpu.roll(b, 8, 1)) for a, b in zip(*rest)])
    for c in range(2):
        across = slice(128 * c, 128 * c + 128)
        plain[at, :, across] = jnp.concatenate(values[0][c] + values[1][c], 0).astype(jnp.bfloat16)
        beside[at, :, across] = jnp.concatenate(sides[0][c] + sides[1][c], 0).astype(jnp.bfloat16)
    ends[at] = jnp.concatenate(rests[0] + rests[1], 0).astype(jnp.bfloat16)


def spread_taps(lines_ref, z, matrix):
    sub, lane = iotas(16)
    diag = (lane & 15) >= sub
    first = iotas(8)[0] < 4
    zero = jnp.zeros((16, 128), jnp.float32)

    def windows(shift):
        found = []
        keep = lane >= sub + 16 * shift
        for p in range(2):
            pair = []
            for e in range(2):
                turned = [zero]
                for v in range(4):
                    row = 4 * (2 * p + e) + v
                    line = jnp.broadcast_to(lines_ref[z, row : row + 1, :], (16, 128))
                    turned.append(pltpu.roll(line, 16 * shift, 1, stride=1, stride_axis=0))
                turned.append(zero)
                pair.append([jnp.where(keep, turned[v + 1], turned[v]) for v in range(5)])
            found.append(pair)
        return found

    start = windows(0)
    here = start
    last = [[jnp.where(diag, start[p][1][3 - di], 0.0) for p in range(2)] for di in range(4)]
    for dx in range(8):
        there = windows(dx + 1) if dx < 7 else start
        for di in range(4):
            v = 4 - di
            u = v if dx < 7 else v - 1
            mid, plus, minus = [], [], []
            for p in range(2):
                mid.append(jnp.where(diag, there[p][0][u], here[p][1][v]))
                plus.append(jnp.where(diag, there[p][1][u], 0.0))
                minus.append(jnp.where(diag, 0.0, here[p][0][v]))
            side = [jnp.concatenate([a[:8], b[8:]], 0) for a, b in zip(plus, minus)]
            for k, (real, imag) in enumerate((mid, side)):
                at = 640 * di + 256 * k + 16 * dx
                real, imag, back = real.astype(jnp.bfloat16), imag.astype(jnp.bfloat16), (-imag).astype(jnp.bfloat16)
                matrix[at : at + 16, 0:128] = real
                matrix[at : at + 16, 128:256] = imag
                matrix[at + 128 : at + 144, 0:128] = back
                matrix[at + 128 : at + 144, 128:256] = real
            at = 640 * di + 512 + 16 * dx
            for k in range(2):
                mine = (minus[k][:8], plus[k][8:])
                crossed = (-last[di][1][8:], -minus[1][:8]) if k == 0 else (last[di][0][8:], minus[0][:8])
                rows = [jnp.where(first, crossed[0], mine[0]), jnp.where(first, mine[1], crossed[1])]
                matrix[at : at + 16, 128 * k : 128 * k + 128] = jnp.concatenate(rows, 0).astype(jnp.bfloat16)
            last[di] = plus
        here = there
        yield


def march_kernel(factor, freq_ref, surface_ref, slow_ref, taps_ref, out_ref,
                 plain0, beside0, ends0, plain1, beside1, ends1, matrix0, matrix1, sums0, sums1,
                 field, slow_raw, slow_own, slow_all, taps_raw, taps_pad, lines, lines_all, image, slots,
                 loaded, local, send, recv, image_send, image_recv):
    me = lax.axis_index("depth")
    freq_at = lax.axis_index("freq")
    waves = ((plain0, beside0, ends0), (plain1, beside1, ends1))
    matrices = (matrix0, matrix1)
    sums = (sums0, sums1)
    margin = REACH * STEPS
    sub, lane = iotas(8)

    taps_load = pltpu.make_async_copy(taps_ref.at[0, 0], taps_raw, loaded.at[0])
    taps_load.start()
    slow_load = pltpu.make_async_copy(slow_ref.at[0], slow_raw, loaded.at[1])
    slow_load.start()

    barrier = pltpu.get_barrier_semaphore()
    for step in range(1, STEPS):
        pl.semaphore_signal(barrier, inc=1, device_id={"depth": lax.rem(me + step, STEPS)}, device_id_type=MESH)
    for k in range(STEPS):
        @pl.when((me != freq_at) | (k != freq_at))
        def _():
            pl.semaphore_signal(barrier, inc=1, device_id={"depth": freq_at, "freq": k}, device_id_type=MESH)

    blank = jnp.zeros((margin, CELLS), field.dtype)
    for w in range(2):
        for c in range(2):
            field[w, c, margin : 2 * margin] = blank
            field[w, c, ROWS + 2 * margin : ROWS + 3 * margin] = blank
    start = pl.multiple_of(jnp.clip(me * ROWS - margin, 0, CELLS - ROWS - 2 * margin), 16)
    offset = pl.multiple_of(start - me * ROWS + 2 * margin, 16)
    surface_loads = [
        pltpu.make_async_copy(
            surface_ref.at[w, 0, c, pl.ds(start, ROWS + 2 * margin)],
            field.at[w, c, pl.ds(offset, ROWS + 2 * margin)], loaded.at[2 + 2 * w + c])
        for w in range(2) for c in range(2)
    ]
    for copy in surface_loads:
        copy.start()

    taps_pad[...] = jnp.zeros_like(taps_pad)
    taps_load.wait()
    row, column = lax.broadcasted_iota(jnp.int32, (128, 256), 0), lax.broadcasted_iota(jnp.int32, (128, 256), 1)
    pick = jnp.where(row == jnp.where(column < 128, 12, 28) - (column & 15), 1.0, 0.0).astype(jnp.bfloat16)
    for p in range(2):
        taps_pad[p, 0:25, 0:25] = taps_raw[p].astype(jnp.float32)
        spread = jnp.dot(taps_pad[p].astype(jnp.bfloat16), pick, preferred_element_type=jnp.float32)
        for e in range(2):
            for v in range(4):
                block = spread[8 * (3 - v) : 8 * (3 - v) + 8, 128 * e : 128 * e + 128]
                block = jnp.where(7 - sub == lane >> 4, block, 0.0)
                at = 4 * (2 * p + e) + v
                lines[at : at + 1, :] = jnp.sum(block, axis=0, keepdims=True)

    pl.semaphore_wait(barrier, 2 * STEPS - 1 - (me == freq_at).astype(jnp.int32))

    taps_copies = [
        pltpu.make_async_remote_copy(
            src_ref=lines, dst_ref=lines_all.at[me], send_sem=send.at[0, step - 1], recv_sem=recv.at[0, step - 1],
            device_id={"depth": lax.rem(me + step, STEPS)}, device_id_type=MESH)
        for step in range(1, STEPS)
    ] + [pltpu.make_async_copy(lines, lines_all.at[me], local.at[0])]
    for copy in taps_copies:
        copy.start()

    def slow_tiles(t):
        return [turn(slow_raw[8 * t : 8 * t + 8, 128 * g : 128 * g + 128] * SCALE) for g in (2, 1, 0)]

    slow_load.wait()
    even = jnp.full((8, 128), me % 2 == 0)
    behind = [jnp.zeros((8, 128), jnp.float32)] * 3

    def place(pair, tiles):
        whole = jnp.round(jnp.concatenate(tiles[0] + tiles[1], 0)).astype(jnp.int32).astype(jnp.int16)
        slow_own[48 * pair : 48 * pair + 48] = whole

    slow_own[: 24 * 4] = jnp.zeros((96, 128), jnp.int16)
    slow_own[24 * 54 :] = jnp.zeros((144, 128), jnp.int16)
    held = [behind]
    for t in range(-1, PLANE_TILES):
        ahead = slow_tiles(t + 1) if t + 1 < PLANE_TILES else behind
        held.append([
            jnp.where(even, pltpu.roll(jnp.where(lane < 64, b, a), 64, 1), a) for a, b in zip(behind, ahead)
        ])
        behind = ahead
        if len(held) == 2:
            place((t + 5) // 2, held)
            held = []

    slow_rows = 24 * WINDOW
    slow_copies = []
    for step in range(1, STEPS):
        other = lax.rem(me + step, STEPS)
        slow_copies.append(pltpu.make_async_remote_copy(
            src_ref=slow_own.at[pl.ds(pl.multiple_of(other * 288, 16), slow_rows)], dst_ref=slow_all.at[me],
            send_sem=send.at[1, step - 1], recv_sem=recv.at[1, step - 1],
            device_id={"depth": other}, device_id_type=MESH))
    slow_copies.append(pltpu.make_async_copy(
        slow_own.at[pl.ds(pl.multiple_of(me * 288, 16), slow_rows)], slow_all.at[me], local.at[1]))
    for copy in slow_copies:
        copy.start()

    for copy in surface_loads:
        copy.wait()

    @pl.loop(0, WINDOW // 2)
    def _(pair):
        both = []
        for w in range(2):
            for c in range(2):
                both.append(field[w, c, pl.ds(pl.multiple_of(margin + 16 * pair, 16), 16), :].astype(jnp.float32))
        for k in range(2):
            tiles = [turn(block[8 * k : 8 * k + 8, 128 * g : 128 * g + 128]) for block in both for g in (2, 1, 0)]
            emit(waves[0], 2 * pair + k, [[tiles[6 * w + 3 * c : 6 * w + 3 * c + 3] for c in range(2)] for w in range(2)])

    for copy in taps_copies:
        copy.wait()
    for _ in spread_taps(lines_all, 0, matrices[0]):
        pass

    freq = freq_ref[0].astype(jnp.float32) * (0.5 / SCALE)

    def outgoing(z):
        return pltpu.make_async_remote_copy(
            src_ref=image.at[z], dst_ref=slots.at[freq_at],
            send_sem=image_send.at[z], recv_sem=image_recv.at[freq_at],
            device_id={"depth": z, "freq": me}, device_id_type=MESH)

    def incoming(k):
        return pltpu.make_async_remote_copy(
            src_ref=image.at[k], dst_ref=slots.at[k],
            send_sem=image_send.at[k], recv_sem=image_recv.at[k],
            device_id={"depth": k, "freq": me}, device_id_type=MESH)

    def convolve_chunk(z, first, size, slot):
        pieces = []
        for di in range(4):
            for ref in waves[z % 2]:
                pieces.append(ref[first + di : first + di + size].reshape(48 * size, ref.shape[2]))
        sums[slot][: 48 * size] = jnp.dot(
            jnp.concatenate(pieces, 1), matrices[z % 2][...], preferred_element_type=jnp.float32)

    products = {}

    def finish_tile(z, i, at, slot):
        halo = REACH * (STEPS - 1 - z)
        base = (margin - REACH * (z + 1)) % 8
        place = i + (1, 3, 4, 6)[z]
        pair = slow_all[z, 48 * (place // 2) : 48 * (place // 2) + 48].astype(jnp.int32)
        half = pair[24 * (place % 2) : 24 * (place % 2) + 24].astype(jnp.float32) * freq
        sine, cosine = rotor(half)
        if 8 * i < halo or 8 * i + 8 > ROWS + halo:
            x = (lane >> 4) + (me * ROWS - halo + 8 * i)
            inside = (x >= 0) & (x < CELLS)
        else:
            inside = None
        values = [[[], []], [[], []]]
        for g in range(3):
            s, c = sine[8 * g : 8 * g + 8], cosine[8 * g : 8 * g + 8]
            if inside is not None:
                s, c = jnp.where(inside, s, 0.0), jnp.where(inside, c, 0.0)
            for w in range(2):
                rows = slice(48 * at + 24 * w + 8 * g, 48 * at + 24 * w + 8 * g + 8)
                real, imag = sums[slot][rows, 0:128], sums[slot][rows, 128:256]
                for k, value in enumerate((real * c - imag * s, real * s + imag * c)):
                    values[w][k].append(value.astype(jnp.bfloat16).astype(jnp.float32))
        if z + 1 < STEPS:
            emit(waves[(z + 1) % 2], i, values)
        if 8 * i + 8 > halo and 8 * i < ROWS + halo:
            (a, b), (c, d) = values
            products[z, i] = [a[g] * c[g] + b[g] * d[g] for g in range(3)]
        whole = halo % 8 == 0
        t = i - halo // 8 if whole else i - halo // 8 - 1
        if 0 <= t < ROWS // 8:
            here = products[z, i]
            if not whole:
                here = [pltpu.roll(jnp.where(lane < 64, b, a), 64, 1) for a, b in zip(products[z, i - 1], here)]
            held_image[t] = here
            if t % 2 == 1:
                image[z, 24 * (t - 1) : 24 * (t + 1)] = jnp.concatenate(held_image.pop(t - 1) + held_image.pop(t), 0).astype(image.dtype)

    held_image = {}
    chunks = [(z, first, size) for z, size in enumerate((7, 6, 5, 4)) for first in range(0, 3 * size, size)]
    waited = set()
    build = iter(())
    for n in range(len(chunks) + 1):
        if n < len(chunks):
            z, first, size = chunks[n]
            if first == 0 and z + 1 < STEPS:
                build = spread_taps(lines_all, z + 1, matrices[(z + 1) % 2])
            convolve_chunk(z, first, size, n % 2)
            for _ in range(4):
                next(build, None)
        if n > 0:
            z, first, size = chunks[n - 1]
            if z == 0 and first == 0:
                for copy in slow_copies:
                    copy.wait()
            for k in range(size):
                finish_tile(z, first + k, k, (n - 1) % 2)
            if first == 2 * size:
                @pl.when((me != freq_at) | (z != me))
                def _():
                    outgoing(z).start()

    own = pltpu.make_async_copy(image.at[me], slots.at[freq_at], local.at[2])

    @pl.when(me == freq_at)
    def _():
        own.start()
        own.wait()

    for k in range(STEPS):
        @pl.when((me != freq_at) | (k != freq_at))
        def _():
            incoming(k).wait_recv()
    for t in range(0, ROWS // 8, 2):
        total = slots[0, 24 * t : 24 * t + 48].astype(jnp.float32)
        for k in range(1, STEPS):
            total = total + slots[k, 24 * t : 24 * t + 48].astype(jnp.float32)
        total = total * factor
        for k in range(2):
            for g in range(3):
                block = total[24 * k + 8 * g : 24 * k + 8 * g + 8]
                out_ref[0, 8 * (t + k) : 8 * (t + k) + 8, 128 * (2 - g) : 128 * (3 - g)] = turn_back(block)
    for k in range(STEPS):
        @pl.when((me != freq_at) | (k != me))
        def _():
            outgoing(k).wait_send()


def march(freq, surface, slow, taps, factor):
    tile = [pltpu.VMEM((WINDOW, 48, lanes), jnp.bfloat16) for lanes in (256, 256, 128)]
    peers = STEPS - 1
    return pl.pallas_call(
        functools.partial(march_kernel, factor),
        out_shape=jax.ShapeDtypeStruct((1, ROWS, CELLS), jnp.float32),
        in_specs=[pl.BlockSpec(memory_space=pltpu.SMEM)] + [pl.BlockSpec(memory_space=pl.ANY)] * 3,
        out_specs=pl.BlockSpec(memory_space=pltpu.VMEM),
        scratch_shapes=tile + tile + [
            pltpu.VMEM((2560, 256), jnp.bfloat16),
            pltpu.VMEM((2560, 256), jnp.bfloat16),
            pltpu.VMEM((336, 256), jnp.float32),
            pltpu.VMEM((336, 256), jnp.float32),
            pltpu.VMEM((2, 2, ROWS + 4 * REACH * STEPS, CELLS), jnp.bfloat16),
            pltpu.VMEM((CELLS, CELLS), jnp.float32),
            pltpu.VMEM((24 * 60, 128), jnp.int16),
            pltpu.VMEM((STEPS, 24 * WINDOW, 128), jnp.int16),
            pltpu.VMEM((2, 25, 25), jnp.bfloat16),
            pltpu.VMEM((2, 32, 128), jnp.float32),
            pltpu.VMEM((16, 128), jnp.float32),
            pltpu.VMEM((STEPS, 16, 128), jnp.float32),
            pltpu.VMEM((STEPS, 288, 128), jnp.bfloat16),
            pltpu.VMEM((STEPS, 288, 128), jnp.bfloat16),
            pltpu.SemaphoreType.DMA((6,)),
            pltpu.SemaphoreType.DMA((3,)),
            pltpu.SemaphoreType.DMA((2, peers)),
            pltpu.SemaphoreType.DMA((2, peers)),
            pltpu.SemaphoreType.DMA((STEPS,)),
            pltpu.SemaphoreType.DMA((STEPS,)),
        ],
        compiler_params=pltpu.CompilerParams(collective_id=0, has_side_effects=True, vmem_limit_bytes=48 << 20),
    )(freq, surface, slow, taps)


def on_device_fused(surface, kernels, slowness, freq_index):
    fixed = (2, 1, 2, CELLS, CELLS) == surface.shape and kernels.shape == (1, 1, 2, 25, 25)
    if not fixed:
        return on_device_general(surface, kernels, slowness, freq_index)
    factor = 1.0 / math.sqrt(lax.axis_size("freq"))
    return march(freq_index, surface, slowness, kernels, factor)


def fits(mesh):
    return mesh.shape["depth"] == 4 and mesh.shape["freq"] == 4


def solution(mesh):
    in_specs = (
        P("shots", "freq", None, None, None),
        P("depth", "freq", None, None, None),
        P("depth", None, None),
        P("freq"),
    )
    out_specs = P(("shots", "depth"), "freq", None)
    body = on_device_fused if fits(mesh) else on_device_general
    return jax.shard_map(
        body, mesh=mesh, in_specs=in_specs, out_specs=out_specs, check_vma=False
    )
```

```python
import functools
import math

import jax
import jax.numpy as jnp
from jax import lax
from jax.experimental import pallas as pl
from jax.experimental.pallas import tpu as pltpu
from jax.sharding import PartitionSpec as P


def with_halo(shard, sides, width):
    for axis, dim in sides:
        size, length = (lax.axis_size(axis), shard.shape[dim])
        up = [(i, (i + 1) % size) for i in range(size - 1)]
        down = [(j, i) for i, j in up]
        last = lax.slice_in_dim(shard, length - width, length, axis=dim)
        leading = lax.slice_in_dim(shard, 0, width, axis=dim)
        before = lax.ppermute(last, axis, up)
        after = lax.ppermute(leading, axis, down)
        shard = jnp.concatenate([before, shard, after], axis=dim)
    return shard


def convolve(padded, stencil, margin):
    rows_in = padded.shape[3]
    cells_y = padded.shape[4]
    tap_count = stencil.shape[-1]
    rows_out = rows_in - 2 * margin
    real_part = stencil[:, 0].astype(jnp.float32)
    imag_part = stencil[:, 1].astype(jnp.float32)
    filters = jnp.stack(
        [jnp.stack([real_part, -imag_part], 1), jnp.stack([imag_part, real_part], 1)], 1
    )
    offsets = lax.iota(jnp.int32, rows_in)[None, :] - lax.iota(jnp.int32, rows_out)[:, None]
    select = (offsets[None] == lax.iota(jnp.int32, tap_count)[:, None, None]).astype(jnp.float32)
    banded = jnp.einsum("fdcab,axk->fdxbck", filters, select).astype(jnp.bfloat16)
    widened = jnp.pad(padded, ((0, 0), (0, 0), (0, 0), (0, 0), (margin, margin)))
    patches = jnp.stack(
        [widened[:, :, :, :, shift : shift + cells_y] for shift in range(tap_count)], 0
    )
    return jnp.einsum("bwfcky,fdxbck->wfdxy", patches, banded, preferred_element_type=jnp.float32)


def rotate(convolved, phase_rate, freq_bins):
    phases = freq_bins[:, None, None] * phase_rate[None]
    cosines = jnp.cos(phases)
    sine_terms = jnp.sin(phases)
    real_out = convolved[:, :, 0] * cosines - convolved[:, :, 1] * sine_terms
    imag_out = convolved[:, :, 0] * sine_terms + convolved[:, :, 1] * cosines
    return jnp.stack([real_out, imag_out], 2).astype(jnp.bfloat16)


def correlate(stepped):
    widened = stepped.astype(jnp.float32)
    return jnp.sum(
        widened[0, :, 0] * widened[1, :, 0] + widened[0, :, 1] * widened[1, :, 1], axis=0
    )


def on_device_general(surface, kernels, slowness, freq_index):
    depth_count = lax.axis_size("depth")
    position = lax.axis_index("depth")
    cells_x = surface.shape[3]
    row_count = cells_x // depth_count
    tap_count = kernels.shape[-1]
    margin = (tap_count - 1) // 2
    start_row = position * row_count
    wavefield = lax.dynamic_slice_in_dim(surface, start_row, row_count, 3)
    stencils = lax.all_gather(kernels, "depth", axis=0, tiled=True)
    phase_rates = lax.all_to_all(slowness, "depth", split_axis=1, concat_axis=0, tiled=True)
    freq_bins = freq_index.astype(jnp.float32)

    def advance(wave, operands):
        stencil, phase_rate = operands
        padded = with_halo(wave, (("depth", 3),), margin)
        stepped = rotate(convolve(padded, stencil, margin), phase_rate, freq_bins)
        return (stepped, correlate(stepped))

    final_wave, partials = lax.scan(advance, wavefield, (stencils, phase_rates))
    moved = lax.all_to_all(partials, "depth", split_axis=0, concat_axis=1, tiled=True)
    summed = lax.psum_scatter(moved, "freq", scatter_dimension=1, tiled=True)
    return summed * (1.0 / math.sqrt(surface.shape[1] * lax.axis_size("freq")))


MESH = pl.DeviceIdType.MESH
SCALE = 32767.0 / 0.02
TX, TY, REACH, STEPS, ROWS, CELLS = 8, 16, 12, 4, 96, 384
PLANE_TILES = CELLS // TX
PIECES = (((0, 8), (8, 16), (16, 22)), ((2, 22),), ((4, 20),), ((6, 18),))
WINDOW = (ROWS + 2 * REACH * STEPS) // TX
SINE = (1.414213201146787, -0.23570044870069473, 0.011782564917166203, -0.00027913063632810375, 3.524705887741897e-06)
COSINE = (1.4142128454174687, -0.7070977888086795, 0.0589074886457319, -0.0019514243489185956, 3.136662365288423e-05)


def iotas(rows):
    return (lax.broadcasted_iota(jnp.int32, (rows, 128), 0), lax.broadcasted_iota(jnp.int32, (rows, 128), 1))


def turn(block):
    group = iotas(8)[1] >> 4
    block = pltpu.roll(block, 16, 1, stride=16, stride_axis=0)
    for k in range(3):
        block = jnp.where((group >> k) & 1 == 1, pltpu.roll(block, 8 - (1 << k), 0), block)
    return pltpu.roll(block, 0, 1, stride=16, stride_axis=0)


def turn_back(block):
    sub, lane = iotas(8)
    group = lane >> 4
    for k in range(3):
        block = jnp.where((sub >> k) & 1 == 1, pltpu.roll(block, 128 - (16 << k), 1), block)
    for k in range(3):
        block = jnp.where((group >> k) & 1 == 1, pltpu.roll(block, 1 << k, 0), block)
    block = pltpu.roll(block, 112, 1)
    for k in range(3):
        block = jnp.where((sub >> k) & 1 == 1, pltpu.roll(block, 128 - (16 << k), 1), block)
    return block


def rotor(phase_half):
    sq = phase_half * phase_half
    sine = jnp.full_like(sq, SINE[-1])
    for value in SINE[-2::-1]:
        sine = sine * sq + value
    sine = sine * phase_half
    cosine = jnp.full_like(sq, COSINE[-1])
    for value in COSINE[-2::-1]:
        cosine = cosine * sq + value
    return sine * cosine, 1.0 - sine * sine


def emit(wave, at, values):
    plain, beside, ends = wave
    sub, lane = iotas(8)
    dy = lane & 15
    low = dy < 8
    middle = (dy >= 4) & (dy < 12)
    sides, rests = [], []
    for w in range(2):
        side, rest = [], []
        for c in range(2):
            v = values[w][c]
            down = [pltpu.roll(x, 1, 0) for x in v]
            up = [pltpu.roll(x, 7, 0) for x in v]
            after = [jnp.where(sub == 0, down[g - 1] if g else 0.0, down[g]) for g in range(3)]
            before = [jnp.where(sub == 7, up[g + 1] if g < 2 else 0.0, up[g]) for g in range(3)]
            side.append([jnp.where(low, a, b) for a, b in zip(after, before)])
            rest.append([jnp.where(low, b, a) for a, b in zip(after, before)])
        sides.append(side)
        rests.append([jnp.where(middle, a, pltpu.roll(b, 8, 1)) for a, b in zip(*rest)])
    for c in range(2):
        across = slice(128 * c, 128 * c + 128)
        plain[at, :, across] = jnp.concatenate(values[0][c] + values[1][c], 0).astype(jnp.bfloat16)
        beside[at, :, across] = jnp.concatenate(sides[0][c] + sides[1][c], 0).astype(jnp.bfloat16)
    ends[at] = jnp.concatenate(rests[0] + rests[1], 0).astype(jnp.bfloat16)


def spread_taps(lines_ref, z, matrix):
    sub, lane = iotas(16)
    diag = (lane & 15) >= sub
    first = iotas(8)[0] < 4
    zero = jnp.zeros((16, 128), jnp.float32)

    def windows(shift):
        found = []
        keep = lane >= sub + 16 * shift
        for p in range(2):
            pair = []
            for e in range(2):
                turned = [zero]
                for v in range(4):
                    row = 4 * (2 * p + e) + v
                    line = jnp.broadcast_to(lines_ref[z, row : row + 1, :], (16, 128))
                    turned.append(pltpu.roll(line, 16 * shift, 1, stride=1, stride_axis=0))
                turned.append(zero)
                pair.append([jnp.where(keep, turned[v + 1], turned[v]) for v in range(5)])
            found.append(pair)
        return found

    start = windows(0)
    here = start
    last = [[jnp.where(diag, start[p][1][3 - di], 0.0) for p in range(2)] for di in range(4)]
    for dx in range(8):
        there = windows(dx + 1) if dx < 7 else start
        for di in range(4):
            v = 4 - di
            u = v if dx < 7 else v - 1
            mid, plus, minus = [], [], []
            for p in range(2):
                mid.append(jnp.where(diag, there[p][0][u], here[p][1][v]))
                plus.append(jnp.where(diag, there[p][1][u], 0.0))
                minus.append(jnp.where(diag, 0.0, here[p][0][v]))
            side = [jnp.concatenate([a[:8], b[8:]], 0) for a, b in zip(plus, minus)]
            for k, (real, imag) in enumerate((mid, side)):
                at = 640 * di + 256 * k + 16 * dx
                real, imag, back = real.astype(jnp.bfloat16), imag.astype(jnp.bfloat16), (-imag).astype(jnp.bfloat16)
                matrix[at : at + 16, 0:128] = real
                matrix[at : at + 16, 128:256] = imag
                matrix[at + 128 : at + 144, 0:128] = back
                matrix[at + 128 : at + 144, 128:256] = real
            at = 640 * di + 512 + 16 * dx
            for k in range(2):
                mine = (minus[k][:8], plus[k][8:])
                crossed = (-last[di][1][8:], -minus[1][:8]) if k == 0 else (last[di][0][8:], minus[0][:8])
                rows = [jnp.where(first, crossed[0], mine[0]), jnp.where(first, mine[1], crossed[1])]
                matrix[at : at + 16, 128 * k : 128 * k + 128] = jnp.concatenate(rows, 0).astype(jnp.bfloat16)
            last[di] = plus
        here = there
        yield


def swap(position):
    return 2 * (position % 2) + position // 2


def lateral(depth, freq):
    return swap(lax.rem(depth + 2 * freq, STEPS))


def march_kernel(factor, freq_ref, surface_ref, slow_ref, taps_ref, out_ref,
                 plain0, beside0, ends0, plain1, beside1, ends1, matrix0, matrix1, sums0, sums1,
                 field, slow_raw, slow_own, slow_all, taps_raw, taps_pad, lines, lines_all, image, slots,
                 loaded, local, send, recv, slow_send, slow_recv, image_send, image_recv):
    me = lax.axis_index("depth")
    freq_at = lax.axis_index("freq")
    lat = lateral(me, freq_at)
    waves = ((plain0, beside0, ends0), (plain1, beside1, ends1))
    matrices = (matrix0, matrix1)
    sums = (sums0, sums1)
    margin = REACH * STEPS
    sub, lane = iotas(8)

    taps_load = pltpu.make_async_copy(taps_ref.at[0, 0], taps_raw, loaded.at[0])
    taps_load.start()
    slow_load = pltpu.make_async_copy(slow_ref.at[0], slow_raw, loaded.at[1])
    slow_load.start()

    barrier = pltpu.get_barrier_semaphore()
    for step in range(1, STEPS):
        pl.semaphore_signal(barrier, inc=1, device_id={"depth": lax.rem(me + step, STEPS)}, device_id_type=MESH)
    for k in range(STEPS):
        @pl.when((lat != freq_at) | (k != freq_at))
        def _():
            source = lax.rem(swap(freq_at) + 2 * k, STEPS)
            pl.semaphore_signal(barrier, inc=1, device_id={"depth": source, "freq": k}, device_id_type=MESH)

    blank = jnp.zeros((margin, CELLS), field.dtype)
    for w in range(2):
        for c in range(2):
            field[w, c, margin : 2 * margin] = blank
            field[w, c, ROWS + 2 * margin : ROWS + 3 * margin] = blank
    start = pl.multiple_of(jnp.clip(lat * ROWS - margin, 0, CELLS - ROWS - 2 * margin), 16)
    offset = pl.multiple_of(start - lat * ROWS + 2 * margin, 16)
    surface_loads = [
        pltpu.make_async_copy(
            surface_ref.at[w, 0, c, pl.ds(start, ROWS + 2 * margin)],
            field.at[w, c, pl.ds(offset, ROWS + 2 * margin)], loaded.at[2 + 2 * w + c])
        for w in range(2) for c in range(2)
    ]
    for copy in surface_loads:
        copy.start()

    taps_pad[...] = jnp.zeros_like(taps_pad)
    taps_load.wait()
    row, column = lax.broadcasted_iota(jnp.int32, (128, 256), 0), lax.broadcasted_iota(jnp.int32, (128, 256), 1)
    pick = jnp.where(row == jnp.where(column < 128, 12, 28) - (column & 15), 1.0, 0.0).astype(jnp.bfloat16)
    for a in range(25):
        taps_pad[2 * a : 2 * a + 2, 0:25] = taps_raw[a].astype(jnp.float32)
    spread = jnp.dot(taps_pad[...].astype(jnp.bfloat16), pick, preferred_element_type=jnp.float32)
    sub16, lane16 = iotas(16)
    for p in range(2):
        chosen = ((sub16 & 1) == p) & (7 - (sub16 >> 1) == lane16 >> 4)
        for e in range(2):
            for v in range(4):
                block = spread[16 * (3 - v) : 16 * (3 - v) + 16, 128 * e : 128 * e + 128]
                at = 4 * (2 * p + e) + v
                lines[at : at + 1, :] = jnp.sum(jnp.where(chosen, block, 0.0), axis=0, keepdims=True)

    pl.semaphore_wait(barrier, 2 * STEPS - 1 - (lat == freq_at).astype(jnp.int32))

    taps_copies = [
        pltpu.make_async_remote_copy(
            src_ref=lines, dst_ref=lines_all.at[me], send_sem=send.at[step - 1], recv_sem=recv.at[step - 1],
            device_id={"depth": lax.rem(me + step, STEPS)}, device_id_type=MESH)
        for step in range(1, STEPS)
    ] + [pltpu.make_async_copy(lines, lines_all.at[me], local.at[0])]
    for copy in taps_copies:
        copy.start()

    def slow_tiles(t):
        return [turn(slow_raw[8 * t : 8 * t + 8, 128 * g : 128 * g + 128] * SCALE) for g in (2, 1, 0)]

    slow_load.wait()
    even = jnp.full((8, 128), me % 2 == 0)
    behind = [jnp.zeros((8, 128), jnp.float32)] * 3

    def place(pair, tiles):
        whole = jnp.round(jnp.concatenate(tiles[0] + tiles[1], 0)).astype(jnp.int32).astype(jnp.int16)
        slow_own[48 * pair : 48 * pair + 48] = whole

    slow_own[: 24 * 4] = jnp.zeros((96, 128), jnp.int16)
    slow_own[24 * 54 :] = jnp.zeros((144, 128), jnp.int16)
    held = [behind]
    for t in range(-1, PLANE_TILES):
        ahead = slow_tiles(t + 1) if t + 1 < PLANE_TILES else behind
        held.append([
            jnp.where(even, pltpu.roll(jnp.where(lane < 64, b, a), 64, 1), a) for a, b in zip(behind, ahead)
        ])
        behind = ahead
        if len(held) == 2:
            place((t + 5) // 2, held)
            held = []

    def slow_copies(z):
        pieces = []
        for n, (low, high) in enumerate(PIECES[z]):
            copies = []
            for step in range(STEPS):
                other = lax.rem(z + step, STEPS)
                at = pl.multiple_of(lateral(other, freq_at) * 288 + 24 * low, 16)
                source = slow_own.at[pl.ds(at, 24 * (high - low))]
                target = slow_all.at[z, 24 * low : 24 * high]
                if step:
                    copies.append(pltpu.make_async_remote_copy(
                        src_ref=source, dst_ref=target, send_sem=slow_send.at[n, step], recv_sem=slow_recv.at[z, n],
                        device_id={"depth": other}, device_id_type=MESH))
                else:
                    copies.append(pltpu.make_async_copy(source, target, slow_recv.at[z, n]))
            pieces.append(copies)
        return pieces

    def start_slow(z):
        @pl.when(me == z)
        def _():
            for copies in slow_copies(z):
                for copy in copies:
                    copy.start()

    def wait_slow(z, n):
        slow_copies(z)[n][0].wait()

    for z in range(0, STEPS, 2):
        start_slow(z)

    for copy in surface_loads:
        copy.wait()

    @pl.loop(0, WINDOW // 2)
    def _(pair):
        both = []
        for w in range(2):
            for c in range(2):
                both.append(field[w, c, pl.ds(pl.multiple_of(margin + 16 * pair, 16), 16), :].astype(jnp.float32))
        for k in range(2):
            tiles = [turn(block[8 * k : 8 * k + 8, 128 * g : 128 * g + 128]) for block in both for g in (2, 1, 0)]
            emit(waves[0], 2 * pair + k, [[tiles[6 * w + 3 * c : 6 * w + 3 * c + 3] for c in range(2)] for w in range(2)])

    for copy in taps_copies:
        copy.wait()
    for _ in spread_taps(lines_all, 0, matrices[0]):
        pass
    for z in range(1, STEPS, 2):
        start_slow(z)

    freq = freq_ref[0].astype(jnp.float32) * (0.5 / SCALE)

    def outgoing(z, k, n):
        low, high = (96 * n, 96 * n + 96) if z == STEPS - 1 else (0, 288)
        return pltpu.make_async_remote_copy(
            src_ref=image.at[z, low:high], dst_ref=slots.at[k, low:high],
            send_sem=image_send.at[z, n], recv_sem=image_recv.at[k, n],
            device_id={"depth": z, "freq": lat}, device_id_type=MESH)

    def send_image(z, n):
        low, high = (96 * n, 96 * n + 96) if z == STEPS - 1 else (0, 288)
        own = (lat == freq_at) & (z == me)

        @pl.when(jnp.logical_not(own))
        def _():
            outgoing(z, freq_at, n).start()

        @pl.when(own)
        def _():
            slots[freq_at, low:high] = image[z, low:high]

    def convolve_chunk(z, first, size, slot):
        pieces = []
        for di in range(4):
            for ref in waves[z % 2]:
                pieces.append(ref[first + di : first + di + size].reshape(48 * size, ref.shape[2]))
        sums[slot][: 48 * size] = jnp.dot(
            jnp.concatenate(pieces, 1), matrices[z % 2][...], preferred_element_type=jnp.float32)

    products = {}

    def finish_tile(z, i, at, slot):
        halo = REACH * (STEPS - 1 - z)
        base = (margin - REACH * (z + 1)) % 8
        place = i + (1, 3, 4, 6)[z]
        pair = slow_all[z, 48 * (place // 2) : 48 * (place // 2) + 48].astype(jnp.int32)
        half = pair[24 * (place % 2) : 24 * (place % 2) + 24].astype(jnp.float32) * freq
        sine, cosine = rotor(half)
        if 8 * i < halo or 8 * i + 8 > ROWS + halo:
            x = (lane >> 4) + (lat * ROWS - halo + 8 * i)
            inside = (x >= 0) & (x < CELLS)
        else:
            inside = None
        values = [[[], []], [[], []]]
        for g in range(3):
            s, c = sine[8 * g : 8 * g + 8], cosine[8 * g : 8 * g + 8]
            if inside is not None:
                s, c = jnp.where(inside, s, 0.0), jnp.where(inside, c, 0.0)
            for w in range(2):
                rows = slice(48 * at + 24 * w + 8 * g, 48 * at + 24 * w + 8 * g + 8)
                real, imag = sums[slot][rows, 0:128], sums[slot][rows, 128:256]
                for k, value in enumerate((real * c - imag * s, real * s + imag * c)):
                    values[w][k].append(value.astype(jnp.bfloat16).astype(jnp.float32))
        if z + 1 < STEPS:
            emit(waves[(z + 1) % 2], i, values)
        if 8 * i + 8 > halo and 8 * i < ROWS + halo:
            (a, b), (c, d) = values
            products[z, i] = [a[g] * c[g] + b[g] * d[g] for g in range(3)]
        whole = halo % 8 == 0
        t = i - halo // 8 if whole else i - halo // 8 - 1
        if 0 <= t < ROWS // 8:
            here = products[z, i]
            if not whole:
                here = [pltpu.roll(jnp.where(lane < 64, b, a), 64, 1) for a, b in zip(products[z, i - 1], here)]
            held_image[t] = here
            if t % 2 == 1:
                image[z, 24 * (t - 1) : 24 * (t + 1)] = jnp.concatenate(held_image.pop(t - 1) + held_image.pop(t), 0).astype(image.dtype)

    held_image = {}
    chunks = [(z, first, size) for z, size in enumerate((7, 6, 5, 4)) for first in range(0, 3 * size, size)]
    waited = set()
    build = iter(())
    for n in range(len(chunks) + 1):
        if n < len(chunks):
            z, first, size = chunks[n]
            if first == 0 and z + 1 < STEPS:
                build = spread_taps(lines_all, z + 1, matrices[(z + 1) % 2])
            convolve_chunk(z, first, size, n % 2)
            for _ in range(4):
                next(build, None)
        if n > 0:
            z, first, size = chunks[n - 1]
            if z == 0 or first == 0:
                wait_slow(z, first // size)
            for k in range(size):
                finish_tile(z, first + k, k, (n - 1) % 2)
            if z == STEPS - 1:
                send_image(z, first // size)
            elif first == 2 * size:
                send_image(z, 0)

    def wait_image(z, n):
        for k in range(STEPS):
            @pl.when((lat != freq_at) | (k != freq_at))
            def _():
                outgoing(z, k, n).wait_recv()

    for n in range(3):
        @pl.when(me == STEPS - 1)
        def _():
            wait_image(STEPS - 1, n)

        if n == 0:
            @pl.when(me != STEPS - 1)
            def _():
                wait_image(0, 0)

        for t in range(4 * n, 4 * n + 4, 2):
            total = slots[0, 24 * t : 24 * t + 48].astype(jnp.float32)
            for k in range(1, STEPS):
                total = total + slots[k, 24 * t : 24 * t + 48].astype(jnp.float32)
            total = total * factor
            for k in range(2):
                for g in range(3):
                    turned = turn_back(total[24 * k + 8 * g : 24 * k + 8 * g + 8])
                    out_ref[0, 8 * (t + k) : 8 * (t + k) + 8, 128 * (2 - g) : 128 * (3 - g)] = turned

    for z in range(STEPS):
        @pl.when((lat != freq_at) | (z != me))
        def _():
            for n in range(3 if z == STEPS - 1 else 1):
                outgoing(z, freq_at, n).wait_send()

        @pl.when(me == z)
        def _():
            for copies in slow_copies(z):
                for copy in copies[1:]:
                    copy.wait_send()


def march(freq, surface, slow, taps, factor):
    tile = [pltpu.VMEM((WINDOW, 48, lanes), jnp.bfloat16) for lanes in (256, 256, 128)]
    peers = STEPS - 1
    return pl.pallas_call(
        functools.partial(march_kernel, factor),
        out_shape=jax.ShapeDtypeStruct((1, ROWS, CELLS), jnp.float32),
        in_specs=[pl.BlockSpec(memory_space=pltpu.SMEM)] + [pl.BlockSpec(memory_space=pl.ANY)] * 3,
        out_specs=pl.BlockSpec(memory_space=pltpu.VMEM),
        scratch_shapes=tile + tile + [
            pltpu.VMEM((2560, 256), jnp.bfloat16),
            pltpu.VMEM((2560, 256), jnp.bfloat16),
            pltpu.VMEM((336, 256), jnp.float32),
            pltpu.VMEM((336, 256), jnp.float32),
            pltpu.VMEM((2, 2, ROWS + 4 * REACH * STEPS, CELLS), jnp.bfloat16),
            pltpu.VMEM((CELLS, CELLS), jnp.float32),
            pltpu.VMEM((24 * 60, 128), jnp.int16),
            pltpu.VMEM((STEPS, 24 * WINDOW, 128), jnp.int16),
            pltpu.VMEM((25, 2, 25), jnp.bfloat16),
            pltpu.VMEM((64, 128), jnp.float32),
            pltpu.VMEM((16, 128), jnp.float32),
            pltpu.VMEM((STEPS, 16, 128), jnp.float32),
            pltpu.VMEM((STEPS, 288, 128), jnp.bfloat16),
            pltpu.VMEM((STEPS, 288, 128), jnp.bfloat16),
            pltpu.SemaphoreType.DMA((6,)),
            pltpu.SemaphoreType.DMA((1,)),
            pltpu.SemaphoreType.DMA((peers,)),
            pltpu.SemaphoreType.DMA((peers,)),
            pltpu.SemaphoreType.DMA((3, STEPS)),
            pltpu.SemaphoreType.DMA((STEPS, 3)),
            pltpu.SemaphoreType.DMA((STEPS, 3)),
            pltpu.SemaphoreType.DMA((STEPS, 3)),
        ],
        compiler_params=pltpu.CompilerParams(collective_id=0, has_side_effects=True, vmem_limit_bytes=107 << 19),
    )(freq, surface, slow, taps)


def on_device_fused(surface, kernels, slowness, freq_index):
    fixed = (2, 1, 2, CELLS, CELLS) == surface.shape and kernels.shape == (1, 1, 2, 25, 25)
    if not fixed:
        return on_device_general(surface, kernels, slowness, freq_index)
    factor = 1.0 / math.sqrt(lax.axis_size("freq"))
    return march(freq_index, surface, slowness, jnp.swapaxes(kernels, 2, 3), factor)


def fits(mesh):
    return mesh.shape["depth"] == 4 and mesh.shape["freq"] == 4


def solution(mesh):
    in_specs = (
        P("shots", "freq", None, None, None),
        P("depth", "freq", None, None, None),
        P("depth", None, None),
        P("freq"),
    )
    out_specs = P(("shots", "depth"), "freq", None)
    body = on_device_fused if fits(mesh) else on_device_general
    return jax.shard_map(
        body, mesh=mesh, in_specs=in_specs, out_specs=out_specs, check_vma=False
    )
```

```python
import functools
import math

import jax
import jax.numpy as jnp
from jax import lax
from jax.experimental import pallas as pl
from jax.experimental.pallas import tpu as pltpu
from jax.sharding import PartitionSpec as P


def with_halo(shard, sides, width):
    for axis, dim in sides:
        size, length = (lax.axis_size(axis), shard.shape[dim])
        up = [(i, (i + 1) % size) for i in range(size - 1)]
        down = [(j, i) for i, j in up]
        last = lax.slice_in_dim(shard, length - width, length, axis=dim)
        leading = lax.slice_in_dim(shard, 0, width, axis=dim)
        before = lax.ppermute(last, axis, up)
        after = lax.ppermute(leading, axis, down)
        shard = jnp.concatenate([before, shard, after], axis=dim)
    return shard


def convolve(padded, stencil, margin):
    rows_in = padded.shape[3]
    cells_y = padded.shape[4]
    tap_count = stencil.shape[-1]
    rows_out = rows_in - 2 * margin
    real_part = stencil[:, 0].astype(jnp.float32)
    imag_part = stencil[:, 1].astype(jnp.float32)
    filters = jnp.stack(
        [jnp.stack([real_part, -imag_part], 1), jnp.stack([imag_part, real_part], 1)], 1
    )
    offsets = lax.iota(jnp.int32, rows_in)[None, :] - lax.iota(jnp.int32, rows_out)[:, None]
    select = (offsets[None] == lax.iota(jnp.int32, tap_count)[:, None, None]).astype(jnp.float32)
    banded = jnp.einsum("fdcab,axk->fdxbck", filters, select).astype(jnp.bfloat16)
    widened = jnp.pad(padded, ((0, 0), (0, 0), (0, 0), (0, 0), (margin, margin)))
    patches = jnp.stack(
        [widened[:, :, :, :, shift : shift + cells_y] for shift in range(tap_count)], 0
    )
    return jnp.einsum("bwfcky,fdxbck->wfdxy", patches, banded, preferred_element_type=jnp.float32)


def rotate(convolved, phase_rate, freq_bins):
    phases = freq_bins[:, None, None] * phase_rate[None]
    cosines = jnp.cos(phases)
    sine_terms = jnp.sin(phases)
    real_out = convolved[:, :, 0] * cosines - convolved[:, :, 1] * sine_terms
    imag_out = convolved[:, :, 0] * sine_terms + convolved[:, :, 1] * cosines
    return jnp.stack([real_out, imag_out], 2).astype(jnp.bfloat16)


def correlate(stepped):
    widened = stepped.astype(jnp.float32)
    return jnp.sum(
        widened[0, :, 0] * widened[1, :, 0] + widened[0, :, 1] * widened[1, :, 1], axis=0
    )


def on_device_general(surface, kernels, slowness, freq_index):
    depth_count = lax.axis_size("depth")
    position = lax.axis_index("depth")
    cells_x = surface.shape[3]
    row_count = cells_x // depth_count
    tap_count = kernels.shape[-1]
    margin = (tap_count - 1) // 2
    start_row = position * row_count
    wavefield = lax.dynamic_slice_in_dim(surface, start_row, row_count, 3)
    stencils = lax.all_gather(kernels, "depth", axis=0, tiled=True)
    phase_rates = lax.all_to_all(slowness, "depth", split_axis=1, concat_axis=0, tiled=True)
    freq_bins = freq_index.astype(jnp.float32)

    def advance(wave, operands):
        stencil, phase_rate = operands
        padded = with_halo(wave, (("depth", 3),), margin)
        stepped = rotate(convolve(padded, stencil, margin), phase_rate, freq_bins)
        return (stepped, correlate(stepped))

    final_wave, partials = lax.scan(advance, wavefield, (stencils, phase_rates))
    moved = lax.all_to_all(partials, "depth", split_axis=0, concat_axis=1, tiled=True)
    summed = lax.psum_scatter(moved, "freq", scatter_dimension=1, tiled=True)
    return summed * (1.0 / math.sqrt(surface.shape[1] * lax.axis_size("freq")))


MESH = pl.DeviceIdType.MESH
SCALE = 32767.0 / 0.02
TX, TY, REACH, STEPS, ROWS, CELLS = 8, 16, 12, 4, 96, 384
PLANE_TILES = CELLS // TX
PIECES = (((0, 80), (80, 128), (128, 192)), ((16, 176),), ((32, 160),), ((48, 144),))
WINDOW = (ROWS + 2 * REACH * STEPS) // TX
SINE = (1.414213201146787, -0.23570044870069473, 0.011782564917166203, -0.00027913063632810375, 3.524705887741897e-06)
COSINE = (1.4142128454174687, -0.7070977888086795, 0.0589074886457319, -0.0019514243489185956, 3.136662365288423e-05)


def iotas(rows):
    return (lax.broadcasted_iota(jnp.int32, (rows, 128), 0), lax.broadcasted_iota(jnp.int32, (rows, 128), 1))


def turn(block):
    group = iotas(8)[1] >> 4
    block = pltpu.roll(block, 16, 1, stride=16, stride_axis=0)
    for k in range(3):
        block = jnp.where((group >> k) & 1 == 1, pltpu.roll(block, 8 - (1 << k), 0), block)
    return pltpu.roll(block, 0, 1, stride=16, stride_axis=0)


def turn_back(block):
    return turn(turn(turn(block)))


def rotor(phase_half):
    sq = phase_half * phase_half
    sine = jnp.full_like(sq, SINE[-1])
    for value in SINE[-2::-1]:
        sine = sine * sq + value
    sine = sine * phase_half
    cosine = jnp.full_like(sq, COSINE[-1])
    for value in COSINE[-2::-1]:
        cosine = cosine * sq + value
    return sine * cosine, 1.0 - sine * sine


def emit(wave, at, values):
    plain, beside, ends = wave
    sub, lane = iotas(8)
    dy = lane & 15
    low = dy < 8
    middle = (dy >= 4) & (dy < 12)
    sides, rests = [], []
    for w in range(2):
        side, rest = [], []
        for c in range(2):
            v = values[w][c]
            down = [pltpu.roll(x, 1, 0) for x in v]
            up = [pltpu.roll(x, 7, 0) for x in v]
            after = [jnp.where(sub == 0, down[g - 1] if g else 0.0, down[g]) for g in range(3)]
            before = [jnp.where(sub == 7, up[g + 1] if g < 2 else 0.0, up[g]) for g in range(3)]
            side.append([jnp.where(low, a, b) for a, b in zip(after, before)])
            rest.append([jnp.where(low, b, a) for a, b in zip(after, before)])
        sides.append(side)
        rests.append([jnp.where(middle, a, pltpu.roll(b, 8, 1)) for a, b in zip(*rest)])
    for c in range(2):
        across = slice(128 * c, 128 * c + 128)
        plain[at, :, across] = jnp.concatenate(values[0][c] + values[1][c], 0).astype(jnp.bfloat16)
        beside[at, :, across] = jnp.concatenate(sides[0][c] + sides[1][c], 0).astype(jnp.bfloat16)
    ends[at] = jnp.concatenate(rests[0] + rests[1], 0).astype(jnp.bfloat16)


def spread_taps(taps_ref, padded, pick, matrix):
    sub, lane = iotas(16)
    diag = (lane & 15) >= sub
    first = iotas(8)[0] < 4
    zero = jnp.zeros((16, 128), jnp.float32)
    for a in range(25):
        padded[2 * a : 2 * a + 2, 0:25] = taps_ref[a].astype(jnp.float32)
    spread = jnp.dot(padded[...].astype(jnp.bfloat16), pick[...], preferred_element_type=jnp.float32)
    lines = {}
    for p in range(2):
        chosen = ((sub & 1) == p) & (7 - (sub >> 1) == lane >> 4)
        for e in range(2):
            for v in range(4):
                part = spread[16 * (3 - v) : 16 * (3 - v) + 16, 128 * e : 128 * e + 128]
                line = jnp.sum(jnp.where(chosen, part, 0.0), axis=0, keepdims=True)
                lines[p, e, v] = jnp.broadcast_to(line, (16, 128))
    yield

    def windows(shift):
        found = []
        keep = lane >= sub + 16 * shift
        for p in range(2):
            pair = []
            for e in range(2):
                turned = [zero]
                for v in range(4):
                    turned.append(pltpu.roll(lines[p, e, v], 16 * shift, 1, stride=1, stride_axis=0))
                turned.append(zero)
                pair.append([jnp.where(keep, turned[v + 1], turned[v]) for v in range(5)])
            found.append(pair)
        return found

    start = windows(0)
    here = start
    last = [[jnp.where(diag, start[p][1][3 - di], 0.0) for p in range(2)] for di in range(4)]
    for dx in range(8):
        there = windows(dx + 1) if dx < 7 else start
        for di in range(4):
            v = 4 - di
            u = v if dx < 7 else v - 1
            mid, plus, minus = [], [], []
            for p in range(2):
                mid.append(jnp.where(diag, there[p][0][u], here[p][1][v]))
                plus.append(jnp.where(diag, there[p][1][u], 0.0))
                minus.append(jnp.where(diag, 0.0, here[p][0][v]))
            side = [jnp.concatenate([a[:8], b[8:]], 0) for a, b in zip(plus, minus)]
            for k, (real, imag) in enumerate((mid, side)):
                at = 640 * di + 256 * k + 16 * dx
                real, imag, back = real.astype(jnp.bfloat16), imag.astype(jnp.bfloat16), (-imag).astype(jnp.bfloat16)
                matrix[at : at + 16, 0:128] = real
                matrix[at : at + 16, 128:256] = imag
                matrix[at + 128 : at + 144, 0:128] = back
                matrix[at + 128 : at + 144, 128:256] = real
            at = 640 * di + 512 + 16 * dx
            for k in range(2):
                mine = (minus[k][:8], plus[k][8:])
                crossed = (-last[di][1][8:], -minus[1][:8]) if k == 0 else (last[di][0][8:], minus[0][:8])
                rows = [jnp.where(first, crossed[0], mine[0]), jnp.where(first, mine[1], crossed[1])]
                matrix[at : at + 16, 128 * k : 128 * k + 128] = jnp.concatenate(rows, 0).astype(jnp.bfloat16)
            last[di] = plus
        here = there
        yield


def swap(position):
    return 2 * (position % 2) + position // 2


def lateral(depth, freq):
    return swap(lax.rem(depth + 2 * freq, STEPS))


def march_kernel(factor, freq_ref, surface_ref, slow_ref, taps_ref, out_ref,
                 plain0, beside0, ends0, plain1, beside1, ends1, matrix0, matrix1, sums0, sums1,
                 field, slow_raw, slow_own, slow_all, taps_all, taps_pad, pick, image, slots,
                 loaded, local, send, recv, slow_send, slow_recv, image_send, image_recv):
    me = lax.axis_index("depth")
    freq_at = lax.axis_index("freq")
    lat = lateral(me, freq_at)
    waves = ((plain0, beside0, ends0), (plain1, beside1, ends1))
    matrices = (matrix0, matrix1)
    sums = (sums0, sums1)
    margin = REACH * STEPS
    sub, lane = iotas(8)

    slow_load = pltpu.make_async_copy(slow_ref.at[0], slow_raw, loaded.at[1])
    slow_load.start()

    barrier = pltpu.get_barrier_semaphore()
    for step in range(1, STEPS):
        pl.semaphore_signal(barrier, inc=1, device_id={"depth": lax.rem(me + step, STEPS)}, device_id_type=MESH)
    for k in range(STEPS):
        @pl.when((lat != freq_at) | (k != freq_at))
        def _():
            source = lax.rem(swap(freq_at) + 2 * k, STEPS)
            pl.semaphore_signal(barrier, inc=1, device_id={"depth": source, "freq": k}, device_id_type=MESH)

    blank = jnp.zeros((margin, CELLS), field.dtype)
    for w in range(2):
        for c in range(2):
            field[w, c, margin : 2 * margin] = blank
            field[w, c, ROWS + 2 * margin : ROWS + 3 * margin] = blank
    start = pl.multiple_of(jnp.clip(lat * ROWS - margin, 0, CELLS - ROWS - 2 * margin), 16)
    offset = pl.multiple_of(start - lat * ROWS + 2 * margin, 16)
    surface_loads = [
        pltpu.make_async_copy(
            surface_ref.at[w, 0, c, pl.ds(start, ROWS + 2 * margin)],
            field.at[w, c, pl.ds(offset, ROWS + 2 * margin)], loaded.at[2 + 2 * w + c])
        for w in range(2) for c in range(2)
    ]
    for copy in surface_loads:
        copy.start()

    taps_pad[...] = jnp.zeros_like(taps_pad)
    row, column = lax.broadcasted_iota(jnp.int32, (128, 256), 0), lax.broadcasted_iota(jnp.int32, (128, 256), 1)
    pick[...] = jnp.where(row == jnp.where(column < 128, 12, 28) - (column & 15), 1.0, 0.0).astype(jnp.bfloat16)

    taps_copies = [
        pltpu.make_async_remote_copy(
            src_ref=taps_ref.at[0, 0], dst_ref=taps_all.at[me], send_sem=send.at[step - 1], recv_sem=recv.at[step - 1],
            device_id={"depth": lax.rem(me + step, STEPS)}, device_id_type=MESH)
        for step in range(1, STEPS)
    ] + [pltpu.make_async_copy(taps_ref.at[0, 0], taps_all.at[me], local.at[0])]

    def enter():
        pl.semaphore_wait(barrier, 2 * STEPS - 1 - (lat == freq_at).astype(jnp.int32))
        for copy in taps_copies:
            copy.start()

    @pl.when(me == 0)
    def _():
        enter()

    slow_own[:margin] = jnp.zeros((margin, CELLS), jnp.int16)
    slow_own[margin + CELLS :] = jnp.zeros((margin, CELLS), jnp.int16)
    slow_load.wait()
    for at in range(0, CELLS, 48):
        coded = jnp.round(slow_raw[at : at + 48] * SCALE).astype(jnp.int32).astype(jnp.int16)
        slow_own[margin + at : margin + at + 48] = coded

    def slow_copies(z):
        pieces = []
        for n, (low, high) in enumerate(PIECES[z]):
            copies = []
            for step in range(STEPS):
                other = lax.rem(z + step, STEPS)
                at = pl.multiple_of(lateral(other, freq_at) * ROWS + low, 16)
                source = slow_own.at[pl.ds(at, high - low)]
                target = slow_all.at[z, low:high]
                if step:
                    copies.append(pltpu.make_async_remote_copy(
                        src_ref=source, dst_ref=target, send_sem=slow_send.at[n, step], recv_sem=slow_recv.at[z, n],
                        device_id={"depth": other}, device_id_type=MESH))
                else:
                    copies.append(pltpu.make_async_copy(source, target, slow_recv.at[z, n]))
            pieces.append(copies)
        return pieces

    def start_slow(z):
        @pl.when(me == z)
        def _():
            for copies in slow_copies(z):
                for copy in copies:
                    copy.start()

    def wait_slow(z, n):
        slow_copies(z)[n][0].wait()

    @pl.when(me != 0)
    def _():
        enter()

    for z in range(0, STEPS, 2):
        start_slow(z)

    for copy in surface_loads:
        copy.wait()

    for pair in range(WINDOW // 2):
        rows = slice(margin + 16 * pair, margin + 16 * pair + 16)
        both = [field[w, c, rows, :].astype(jnp.float32) for w in range(2) for c in range(2)]
        for k in range(2):
            tiles = [turn(x[8 * k : 8 * k + 8, 128 * g : 128 * g + 128]) for x in both for g in (2, 1, 0)]
            emit(waves[0], 2 * pair + k, [[tiles[6 * w + 3 * c : 6 * w + 3 * c + 3] for c in range(2)] for w in range(2)])

    for copy in taps_copies:
        copy.wait()
    for _ in spread_taps(taps_all.at[0], taps_pad, pick, matrices[0]):
        pass
    for z in range(1, STEPS, 2):
        start_slow(z)

    freq = freq_ref[0].astype(jnp.float32) * (0.5 / SCALE)

    def outgoing(z, k, n):
        low, high = (96 * n, 96 * n + 96) if z == STEPS - 1 else (0, 288)
        return pltpu.make_async_remote_copy(
            src_ref=image.at[z, low:high], dst_ref=slots.at[k, low:high],
            send_sem=image_send.at[z, n], recv_sem=image_recv.at[k, n],
            device_id={"depth": z, "freq": lat}, device_id_type=MESH)

    def send_image(z, n):
        low, high = (96 * n, 96 * n + 96) if z == STEPS - 1 else (0, 288)
        own = (lat == freq_at) & (z == me)

        @pl.when(jnp.logical_not(own))
        def _():
            outgoing(z, freq_at, n).start()

        @pl.when(own)
        def _():
            slots[freq_at, low:high] = image[z, low:high]

    def convolve_chunk(z, first, size, slot):
        pieces = []
        for di in range(4):
            for ref in waves[z % 2]:
                pieces.append(ref[first + di : first + di + size].reshape(48 * size, ref.shape[2]))
        sums[slot][: 48 * size] = jnp.dot(
            jnp.concatenate(pieces, 1), matrices[z % 2][...], preferred_element_type=jnp.float32)

    products, coded_rows = {}, {}

    def slow_rows(z, n):
        if (z, n // 2) not in coded_rows:
            coded_rows[z, n // 2] = slow_all[z, 16 * (n // 2) : 16 * (n // 2) + 16].astype(jnp.int32).astype(jnp.float32)
            coded_rows.pop((z, n // 2 - 2), None)
        return [coded_rows[z, n // 2][8 * (n % 2) : 8 * (n % 2) + 8, 128 * g : 128 * g + 128] for g in range(3)]

    def finish_tile(z, i, at, slot):
        halo = REACH * (STEPS - 1 - z)
        low = REACH * (z + 1) + 8 * i
        parts = slow_rows(z, low // 8)
        if low % 8:
            parts = [pltpu.roll(jnp.where(sub < 4, b, a), 4, 0) for a, b in zip(parts, slow_rows(z, low // 8 + 1))]
        sine, cosine = rotor(jnp.concatenate([turn(parts[g]) for g in (2, 1, 0)], 0) * freq)
        if 8 * i < halo or 8 * i + 8 > ROWS + halo:
            x = (lane >> 4) + (lat * ROWS - halo + 8 * i)
            inside = (x >= 0) & (x < CELLS)
        else:
            inside = None
        values = [[[], []], [[], []]]
        for g in range(3):
            s, c = sine[8 * g : 8 * g + 8], cosine[8 * g : 8 * g + 8]
            if inside is not None:
                s, c = jnp.where(inside, s, 0.0), jnp.where(inside, c, 0.0)
            for w in range(2):
                rows = slice(48 * at + 24 * w + 8 * g, 48 * at + 24 * w + 8 * g + 8)
                real, imag = sums[slot][rows, 0:128], sums[slot][rows, 128:256]
                for k, value in enumerate((real * c - imag * s, real * s + imag * c)):
                    values[w][k].append(value.astype(jnp.bfloat16).astype(jnp.float32))
        if z + 1 < STEPS:
            emit(waves[(z + 1) % 2], i, values)
        if 8 * i + 8 > halo and 8 * i < ROWS + halo:
            (a, b), (c, d) = values
            products[z, i] = [a[g] * c[g] + b[g] * d[g] for g in range(3)]
        whole = halo % 8 == 0
        t = i - halo // 8 if whole else i - halo // 8 - 1
        if 0 <= t < ROWS // 8:
            here = products[z, i]
            if not whole:
                here = [pltpu.roll(jnp.where(lane < 64, b, a), 64, 1) for a, b in zip(products[z, i - 1], here)]
            held_image[t] = here
            if t % 2 == 1:
                image[z, 24 * (t - 1) : 24 * (t + 1)] = jnp.concatenate(held_image.pop(t - 1) + held_image.pop(t), 0).astype(image.dtype)

    held_image = {}
    chunks = [(z, first, size) for z, size in enumerate((7, 6, 5, 4)) for first in range(0, 3 * size, size)]
    waited = set()
    build = iter(())
    for n in range(len(chunks) + 1):
        if n < len(chunks):
            z, first, size = chunks[n]
            if first == 0 and z + 1 < STEPS:
                build = spread_taps(taps_all.at[z + 1], taps_pad, pick, matrices[(z + 1) % 2])
            convolve_chunk(z, first, size, n % 2)
            for _ in range(4):
                next(build, None)
        if n > 0:
            z, first, size = chunks[n - 1]
            if z == 0 or first == 0:
                wait_slow(z, first // size)
            for k in range(size):
                finish_tile(z, first + k, k, (n - 1) % 2)
            if z == STEPS - 1:
                send_image(z, first // size)
            elif first == 2 * size:
                send_image(z, 0)

    def wait_image(z, n):
        for k in range(STEPS):
            @pl.when((lat != freq_at) | (k != freq_at))
            def _():
                outgoing(z, k, n).wait_recv()

    for n in range(3):
        @pl.when(me == STEPS - 1)
        def _():
            wait_image(STEPS - 1, n)

        if n == 0:
            @pl.when(me != STEPS - 1)
            def _():
                wait_image(0, 0)

        for t in range(4 * n, 4 * n + 4, 2):
            total = slots[0, 24 * t : 24 * t + 48].astype(jnp.float32)
            for k in range(1, STEPS):
                total = total + slots[k, 24 * t : 24 * t + 48].astype(jnp.float32)
            total = total * factor
            for k in range(2):
                for g in range(3):
                    turned = turn_back(total[24 * k + 8 * g : 24 * k + 8 * g + 8])
                    out_ref[0, 8 * (t + k) : 8 * (t + k) + 8, 128 * (2 - g) : 128 * (3 - g)] = turned

    for z in range(STEPS):
        @pl.when((lat != freq_at) | (z != me))
        def _():
            for n in range(3 if z == STEPS - 1 else 1):
                outgoing(z, freq_at, n).wait_send()

        @pl.when(me == z)
        def _():
            for copies in slow_copies(z):
                for copy in copies[1:]:
                    copy.wait_send()


def march(freq, surface, slow, taps, factor):
    tile = [pltpu.VMEM((WINDOW, 48, lanes), jnp.bfloat16) for lanes in (256, 256, 128)]
    peers = STEPS - 1
    return pl.pallas_call(
        functools.partial(march_kernel, factor),
        out_shape=jax.ShapeDtypeStruct((1, ROWS, CELLS), jnp.float32),
        in_specs=[pl.BlockSpec(memory_space=pltpu.SMEM)] + [pl.BlockSpec(memory_space=pl.ANY)] * 3,
        out_specs=pl.BlockSpec(memory_space=pltpu.VMEM),
        scratch_shapes=tile + tile + [
            pltpu.VMEM((2560, 256), jnp.bfloat16),
            pltpu.VMEM((2560, 256), jnp.bfloat16),
            pltpu.VMEM((336, 256), jnp.float32),
            pltpu.VMEM((336, 256), jnp.float32),
            pltpu.VMEM((2, 2, ROWS + 4 * REACH * STEPS, CELLS), jnp.bfloat16),
            pltpu.VMEM((CELLS, CELLS), jnp.float32),
            pltpu.VMEM((CELLS + 2 * REACH * STEPS, CELLS), jnp.int16),
            pltpu.VMEM((STEPS, ROWS + 2 * REACH * STEPS, CELLS), jnp.int16),
            pltpu.VMEM((STEPS, 25, 2, 25), jnp.bfloat16),
            pltpu.VMEM((64, 128), jnp.float32),
            pltpu.VMEM((128, 256), jnp.bfloat16),
            pltpu.VMEM((STEPS, 288, 128), jnp.bfloat16),
            pltpu.VMEM((STEPS, 288, 128), jnp.bfloat16),
            pltpu.SemaphoreType.DMA((6,)),
            pltpu.SemaphoreType.DMA((1,)),
            pltpu.SemaphoreType.DMA((peers,)),
            pltpu.SemaphoreType.DMA((peers,)),
            pltpu.SemaphoreType.DMA((3, STEPS)),
            pltpu.SemaphoreType.DMA((STEPS, 3)),
            pltpu.SemaphoreType.DMA((STEPS, 3)),
            pltpu.SemaphoreType.DMA((STEPS, 3)),
        ],
        compiler_params=pltpu.CompilerParams(collective_id=0, has_side_effects=True, vmem_limit_bytes=48 << 20),
    )(freq, *(pltpu.with_memory_space_constraint(x, pltpu.HBM) for x in (surface, slow, taps)))


def on_device_fused(surface, kernels, slowness, freq_index):
    fixed = (2, 1, 2, CELLS, CELLS) == surface.shape and kernels.shape == (1, 1, 2, 25, 25)
    if not fixed:
        return on_device_general(surface, kernels, slowness, freq_index)
    factor = 1.0 / math.sqrt(lax.axis_size("freq"))
    return march(freq_index, surface, slowness, jnp.swapaxes(kernels, 2, 3), factor)


def fits(mesh):
    return mesh.shape["depth"] == 4 and mesh.shape["freq"] == 4


def solution(mesh):
    in_specs = (
        P("shots", "freq", None, None, None),
        P("depth", "freq", None, None, None),
        P("depth", None, None),
        P("freq"),
    )
    out_specs = P(("shots", "depth"), "freq", None)
    body = on_device_fused if fits(mesh) else on_device_general
    return jax.shard_map(
        body, mesh=mesh, in_specs=in_specs, out_specs=out_specs, check_vma=False
    )
```

```python
import functools
import math

import jax
import jax.numpy as jnp
from jax import lax
from jax.experimental import pallas as pl
from jax.experimental.pallas import tpu as pltpu
from jax.sharding import PartitionSpec as P


def with_halo(shard, sides, width):
    for axis, dim in sides:
        size, length = (lax.axis_size(axis), shard.shape[dim])
        up = [(i, (i + 1) % size) for i in range(size - 1)]
        down = [(j, i) for i, j in up]
        last = lax.slice_in_dim(shard, length - width, length, axis=dim)
        leading = lax.slice_in_dim(shard, 0, width, axis=dim)
        before = lax.ppermute(last, axis, up)
        after = lax.ppermute(leading, axis, down)
        shard = jnp.concatenate([before, shard, after], axis=dim)
    return shard


def convolve(padded, stencil, margin):
    rows_in = padded.shape[3]
    cells_y = padded.shape[4]
    tap_count = stencil.shape[-1]
    rows_out = rows_in - 2 * margin
    real_part = stencil[:, 0].astype(jnp.float32)
    imag_part = stencil[:, 1].astype(jnp.float32)
    filters = jnp.stack(
        [jnp.stack([real_part, -imag_part], 1), jnp.stack([imag_part, real_part], 1)], 1
    )
    offsets = lax.iota(jnp.int32, rows_in)[None, :] - lax.iota(jnp.int32, rows_out)[:, None]
    select = (offsets[None] == lax.iota(jnp.int32, tap_count)[:, None, None]).astype(jnp.float32)
    banded = jnp.einsum("fdcab,axk->fdxbck", filters, select).astype(jnp.bfloat16)
    widened = jnp.pad(padded, ((0, 0), (0, 0), (0, 0), (0, 0), (margin, margin)))
    patches = jnp.stack(
        [widened[:, :, :, :, shift : shift + cells_y] for shift in range(tap_count)], 0
    )
    return jnp.einsum("bwfcky,fdxbck->wfdxy", patches, banded, preferred_element_type=jnp.float32)


def rotate(convolved, phase_rate, freq_bins):
    phases = freq_bins[:, None, None] * phase_rate[None]
    cosines = jnp.cos(phases)
    sine_terms = jnp.sin(phases)
    real_out = convolved[:, :, 0] * cosines - convolved[:, :, 1] * sine_terms
    imag_out = convolved[:, :, 0] * sine_terms + convolved[:, :, 1] * cosines
    return jnp.stack([real_out, imag_out], 2).astype(jnp.bfloat16)


def correlate(stepped):
    widened = stepped.astype(jnp.float32)
    return jnp.sum(
        widened[0, :, 0] * widened[1, :, 0] + widened[0, :, 1] * widened[1, :, 1], axis=0
    )


def on_device_general(surface, kernels, slowness, freq_index):
    depth_count = lax.axis_size("depth")
    position = lax.axis_index("depth")
    cells_x = surface.shape[3]
    row_count = cells_x // depth_count
    tap_count = kernels.shape[-1]
    margin = (tap_count - 1) // 2
    start_row = position * row_count
    wavefield = lax.dynamic_slice_in_dim(surface, start_row, row_count, 3)
    stencils = lax.all_gather(kernels, "depth", axis=0, tiled=True)
    phase_rates = lax.all_to_all(slowness, "depth", split_axis=1, concat_axis=0, tiled=True)
    freq_bins = freq_index.astype(jnp.float32)

    def advance(wave, operands):
        stencil, phase_rate = operands
        padded = with_halo(wave, (("depth", 3),), margin)
        stepped = rotate(convolve(padded, stencil, margin), phase_rate, freq_bins)
        return (stepped, correlate(stepped))

    final_wave, partials = lax.scan(advance, wavefield, (stencils, phase_rates))
    moved = lax.all_to_all(partials, "depth", split_axis=0, concat_axis=1, tiled=True)
    summed = lax.psum_scatter(moved, "freq", scatter_dimension=1, tiled=True)
    return summed * (1.0 / math.sqrt(surface.shape[1] * lax.axis_size("freq")))


MESH = pl.DeviceIdType.MESH
SCALE = 32767.0 / 0.02
TX, TY, REACH, STEPS, ROWS, CELLS = 8, 16, 12, 4, 96, 384
PLANE_TILES = CELLS // TX
PIECES = (((16, 192),), ((32, 176),), ((32, 176),), ((48, 160),))
IMAGE_PIECES = (((0, 288),),) * 3 + (((0, 192), (192, 288)),)
LEAD = REACH * STEPS + 8
WINDOW = (ROWS + 2 * REACH * STEPS) // TX
SINE = (1.414213201146787, -0.23570044870069473, 0.011782564917166203, -0.00027913063632810375, 3.524705887741897e-06)
COSINE = (1.4142128454174687, -0.7070977888086795, 0.0589074886457319, -0.0019514243489185956, 3.136662365288423e-05)


def iotas(rows):
    return (lax.broadcasted_iota(jnp.int32, (rows, 128), 0), lax.broadcasted_iota(jnp.int32, (rows, 128), 1))


def turn(block):
    group = iotas(8)[1] >> 4
    block = pltpu.roll(block, 16, 1, stride=16, stride_axis=0)
    for k in range(3):
        block = jnp.where((group >> k) & 1 == 1, pltpu.roll(block, 8 - (1 << k), 0), block)
    return pltpu.roll(block, 0, 1, stride=16, stride_axis=0)


def turn_back(block):
    return turn(turn(turn(block)))


def rotor(phase_half):
    sq = phase_half * phase_half
    sine = jnp.full_like(sq, SINE[-1])
    for value in SINE[-2::-1]:
        sine = sine * sq + value
    sine = sine * phase_half
    cosine = jnp.full_like(sq, COSINE[-1])
    for value in COSINE[-2::-1]:
        cosine = cosine * sq + value
    return sine * cosine, 1.0 - sine * sine


def emit(wave, at, values):
    plain, beside, ends = wave
    sub, lane = iotas(8)
    dy = lane & 15
    low = dy < 8
    middle = (dy >= 4) & (dy < 12)
    sides, rests = [], []
    for w in range(2):
        side, rest = [], []
        for c in range(2):
            v = values[w][c]
            down = [pltpu.roll(x, 1, 0) for x in v]
            up = [pltpu.roll(x, 7, 0) for x in v]
            after = [jnp.where(sub == 0, down[g - 1] if g else 0.0, down[g]) for g in range(3)]
            before = [jnp.where(sub == 7, up[g + 1] if g < 2 else 0.0, up[g]) for g in range(3)]
            side.append([jnp.where(low, a, b) for a, b in zip(after, before)])
            rest.append([jnp.where(low, b, a) for a, b in zip(after, before)])
        sides.append(side)
        rests.append([jnp.where(middle, a, pltpu.roll(b, 8, 1)) for a, b in zip(*rest)])
    for c in range(2):
        across = slice(128 * c, 128 * c + 128)
        plain[at, :, across] = jnp.concatenate(values[0][c] + values[1][c], 0).astype(jnp.bfloat16)
        beside[at, :, across] = jnp.concatenate(sides[0][c] + sides[1][c], 0).astype(jnp.bfloat16)
    ends[at] = jnp.concatenate(rests[0] + rests[1], 0).astype(jnp.bfloat16)


def spread_taps(taps_ref, padded, pick, matrix):
    sub, lane = iotas(16)
    diag = (lane & 15) >= sub
    first = iotas(8)[0] < 4
    zero = jnp.zeros((16, 128), jnp.float32)
    for a in range(25):
        padded[2 * a : 2 * a + 2, 0:25] = taps_ref[a].astype(jnp.float32)
    spread = jnp.dot(padded[...].astype(jnp.bfloat16), pick[...], preferred_element_type=jnp.float32)
    lines = {}
    for p in range(2):
        chosen = ((sub & 1) == p) & (7 - (sub >> 1) == lane >> 4)
        for e in range(2):
            for v in range(4):
                part = spread[16 * (3 - v) : 16 * (3 - v) + 16, 128 * e : 128 * e + 128]
                line = jnp.sum(jnp.where(chosen, part, 0.0), axis=0, keepdims=True)
                lines[p, e, v] = jnp.broadcast_to(line, (16, 128))
    yield

    def windows(shift):
        found = []
        keep = lane >= sub + 16 * shift
        for p in range(2):
            pair = []
            for e in range(2):
                turned = [zero]
                for v in range(4):
                    turned.append(pltpu.roll(lines[p, e, v], 16 * shift, 1, stride=1, stride_axis=0))
                turned.append(zero)
                pair.append([jnp.where(keep, turned[v + 1], turned[v]) for v in range(5)])
            found.append(pair)
        return found

    start = windows(0)
    here = start
    last = [[jnp.where(diag, start[p][1][3 - di], 0.0) for p in range(2)] for di in range(4)]
    for dx in range(8):
        there = windows(dx + 1) if dx < 7 else start
        for di in range(4):
            v = 4 - di
            u = v if dx < 7 else v - 1
            mid, plus, minus = [], [], []
            for p in range(2):
                mid.append(jnp.where(diag, there[p][0][u], here[p][1][v]))
                plus.append(jnp.where(diag, there[p][1][u], 0.0))
                minus.append(jnp.where(diag, 0.0, here[p][0][v]))
            side = [jnp.concatenate([a[:8], b[8:]], 0) for a, b in zip(plus, minus)]
            for k, (real, imag) in enumerate((mid, side)):
                at = 640 * di + 256 * k + 16 * dx
                real, imag, back = real.astype(jnp.bfloat16), imag.astype(jnp.bfloat16), (-imag).astype(jnp.bfloat16)
                matrix[at : at + 16, 0:128] = real
                matrix[at : at + 16, 128:256] = imag
                matrix[at + 128 : at + 144, 0:128] = back
                matrix[at + 128 : at + 144, 128:256] = real
            at = 640 * di + 512 + 16 * dx
            for k in range(2):
                mine = (minus[k][:8], plus[k][8:])
                crossed = (-last[di][1][8:], -minus[1][:8]) if k == 0 else (last[di][0][8:], minus[0][:8])
                rows = [jnp.where(first, crossed[0], mine[0]), jnp.where(first, mine[1], crossed[1])]
                matrix[at : at + 16, 128 * k : 128 * k + 128] = jnp.concatenate(rows, 0).astype(jnp.bfloat16)
            last[di] = plus
        here = there
        yield


def swap(position):
    return 2 * (position % 2) + position // 2


def lateral(depth, freq):
    return swap(lax.rem(depth + 2 * freq, STEPS))


def march_kernel(factor, freq_ref, surface_ref, slow_ref, taps_ref, out_ref,
                 plain0, beside0, ends0, plain1, beside1, ends1, matrix0, matrix1, sums0, sums1,
                 field, slow_raw, slow_own, slow_all, taps_all, taps_pad, pick, image, slots,
                 loaded, local, send, recv, slow_send, slow_recv, image_send, image_recv):
    me = lax.axis_index("depth")
    freq_at = lax.axis_index("freq")
    lat = lateral(me, freq_at)
    waves = ((plain0, beside0, ends0), (plain1, beside1, ends1))
    matrices = (matrix0, matrix1)
    sums = (sums0, sums1)
    margin = REACH * STEPS
    sub, lane = iotas(8)

    slow_load = pltpu.make_async_copy(slow_ref.at[0], slow_raw, loaded.at[1])
    slow_load.start()

    barrier = pltpu.get_barrier_semaphore()
    for step in range(1, STEPS):
        pl.semaphore_signal(barrier, inc=1, device_id={"depth": lax.rem(me + step, STEPS)}, device_id_type=MESH)
    for k in range(STEPS):
        @pl.when((lat != freq_at) | (k != freq_at))
        def _():
            source = lax.rem(swap(freq_at) + 2 * k, STEPS)
            pl.semaphore_signal(barrier, inc=1, device_id={"depth": source, "freq": k}, device_id_type=MESH)

    blank = jnp.zeros((margin, CELLS), field.dtype)
    for w in range(2):
        for c in range(2):
            field[w, c, margin : 2 * margin] = blank
            field[w, c, ROWS + 2 * margin : ROWS + 3 * margin] = blank
    start = pl.multiple_of(jnp.clip(lat * ROWS - margin, 0, CELLS - ROWS - 2 * margin), 16)
    offset = pl.multiple_of(start - lat * ROWS + 2 * margin, 16)
    surface_loads = [
        pltpu.make_async_copy(
            surface_ref.at[w, 0, c, pl.ds(start, ROWS + 2 * margin)],
            field.at[w, c, pl.ds(offset, ROWS + 2 * margin)], loaded.at[2 + 2 * w + c])
        for w in range(2) for c in range(2)
    ]
    for copy in surface_loads:
        copy.start()

    taps_pad[...] = jnp.zeros_like(taps_pad)
    row, column = lax.broadcasted_iota(jnp.int32, (128, 256), 0), lax.broadcasted_iota(jnp.int32, (128, 256), 1)
    pick[...] = jnp.where(row == jnp.where(column < 128, 12, 28) - (column & 15), 1.0, 0.0).astype(jnp.bfloat16)

    taps_copies = [
        pltpu.make_async_remote_copy(
            src_ref=taps_ref.at[0, 0], dst_ref=taps_all.at[me], send_sem=send.at[step - 1], recv_sem=recv.at[step - 1],
            device_id={"depth": lax.rem(me + step, STEPS)}, device_id_type=MESH)
        for step in range(1, STEPS)
    ] + [pltpu.make_async_copy(taps_ref.at[0, 0], taps_all.at[me], local.at[0])]

    def enter():
        pl.semaphore_wait(barrier, 2 * STEPS - 1 - (lat == freq_at).astype(jnp.int32))
        for copy in taps_copies:
            copy.start()

    @pl.when(me == 0)
    def _():
        enter()

    slow_load.wait()
    for at in range(0, slow_own.shape[0], 16):
        halves = [
            jnp.round(slow_raw[low : low + 8] * SCALE) if 0 <= low < CELLS else jnp.zeros((8, CELLS), jnp.float32)
            for low in (at - LEAD, at - LEAD + 8)
        ]
        slow_own[at : at + 16] = jnp.concatenate(halves, 0).astype(jnp.int32).astype(jnp.int16)

    def slow_copies(z):
        pieces = []
        for n, (low, high) in enumerate(PIECES[z]):
            copies = []
            for step in range(STEPS):
                other = lax.rem(z + step, STEPS)
                at = pl.multiple_of(lateral(other, freq_at) * ROWS + low, 16)
                source = slow_own.at[pl.ds(at, high - low)]
                target = slow_all.at[z, low:high]
                if step:
                    copies.append(pltpu.make_async_remote_copy(
                        src_ref=source, dst_ref=target, send_sem=slow_send.at[n, step], recv_sem=slow_recv.at[z, n],
                        device_id={"depth": other}, device_id_type=MESH))
                else:
                    copies.append(pltpu.make_async_copy(source, target, slow_recv.at[z, n]))
            pieces.append(copies)
        return pieces

    def start_slow(z):
        @pl.when(me == z)
        def _():
            for copies in slow_copies(z):
                for copy in copies:
                    copy.start()

    def wait_slow(z, n):
        slow_copies(z)[n][0].wait()

    @pl.when(me != 0)
    def _():
        enter()

    for z in range(0, STEPS, 2):
        start_slow(z)

    for copy in surface_loads:
        copy.wait()

    for pair in range(WINDOW // 2):
        rows = slice(margin + 16 * pair, margin + 16 * pair + 16)
        both = [field[w, c, rows, :].astype(jnp.float32) for w in range(2) for c in range(2)]
        for k in range(2):
            tiles = [turn(x[8 * k : 8 * k + 8, 128 * g : 128 * g + 128]) for x in both for g in (2, 1, 0)]
            emit(waves[0], 2 * pair + k, [[tiles[6 * w + 3 * c : 6 * w + 3 * c + 3] for c in range(2)] for w in range(2)])

    for copy in taps_copies:
        copy.wait()
    for _ in spread_taps(taps_all.at[0], taps_pad, pick, matrices[0]):
        pass
    for z in range(1, STEPS, 2):
        start_slow(z)

    freq = freq_ref[0].astype(jnp.float32) * (0.5 / SCALE)

    def outgoing(z, k, n):
        low, high = IMAGE_PIECES[z][n]
        return pltpu.make_async_remote_copy(
            src_ref=image.at[z, low:high], dst_ref=slots.at[k, low:high],
            send_sem=image_send.at[z, n], recv_sem=image_recv.at[k, n],
            device_id={"depth": z, "freq": lat}, device_id_type=MESH)

    def send_image(z, n):
        low, high = IMAGE_PIECES[z][n]
        own = (lat == freq_at) & (z == me)

        @pl.when(jnp.logical_not(own))
        def _():
            outgoing(z, freq_at, n).start()

        @pl.when(own)
        def _():
            slots[freq_at, low:high] = image[z, low:high]

    def convolve_chunk(z, first, size, slot):
        pieces = []
        for di in range(4):
            for ref in waves[z % 2]:
                pieces.append(ref[first + di : first + di + size].reshape(48 * size, ref.shape[2]))
        sums[slot][: 48 * size] = jnp.dot(
            jnp.concatenate(pieces, 1), matrices[z % 2][...], preferred_element_type=jnp.float32)

    products, coded_rows = {}, {}

    def slow_rows(z, n):
        if (z, n // 2) not in coded_rows:
            coded_rows[z, n // 2] = slow_all[z, 16 * (n // 2) : 16 * (n // 2) + 16].astype(jnp.int32).astype(jnp.float32)
            coded_rows.pop((z, n // 2 - 2), None)
        return [coded_rows[z, n // 2][8 * (n % 2) : 8 * (n % 2) + 8, 128 * g : 128 * g + 128] for g in range(3)]

    def finish_tile(z, i, at, slot):
        halo = REACH * (STEPS - 1 - z)
        low = LEAD - REACH * (STEPS - 1 - z) + 8 * i
        parts = slow_rows(z, low // 8)
        if low % 8:
            parts = [pltpu.roll(jnp.where(sub < 4, b, a), 4, 0) for a, b in zip(parts, slow_rows(z, low // 8 + 1))]
        sine, cosine = rotor(jnp.concatenate([turn(parts[g]) for g in (2, 1, 0)], 0) * freq)
        if 8 * i < halo or 8 * i + 8 > ROWS + halo:
            x = (lane >> 4) + (lat * ROWS - halo + 8 * i)
            inside = (x >= 0) & (x < CELLS)
        else:
            inside = None
        values = [[[], []], [[], []]]
        for g in range(3):
            s, c = sine[8 * g : 8 * g + 8], cosine[8 * g : 8 * g + 8]
            if inside is not None:
                s, c = jnp.where(inside, s, 0.0), jnp.where(inside, c, 0.0)
            for w in range(2):
                rows = slice(48 * at + 24 * w + 8 * g, 48 * at + 24 * w + 8 * g + 8)
                real, imag = sums[slot][rows, 0:128], sums[slot][rows, 128:256]
                for k, value in enumerate((real * c - imag * s, real * s + imag * c)):
                    values[w][k].append(value.astype(jnp.bfloat16).astype(jnp.float32))
        if z + 1 < STEPS:
            emit(waves[(z + 1) % 2], i, values)
        if 8 * i + 8 > halo and 8 * i < ROWS + halo:
            (a, b), (c, d) = values
            products[z, i] = [a[g] * c[g] + b[g] * d[g] for g in range(3)]
        whole = halo % 8 == 0
        t = i - halo // 8 if whole else i - halo // 8 - 1
        if 0 <= t < ROWS // 8:
            here = products[z, i]
            if not whole:
                here = [pltpu.roll(jnp.where(lane < 64, b, a), 64, 1) for a, b in zip(products[z, i - 1], here)]
            held_image[t] = here
            if t % 2 == 1:
                image[z, 24 * (t - 1) : 24 * (t + 1)] = jnp.concatenate(held_image.pop(t - 1) + held_image.pop(t), 0).astype(image.dtype)

    held_image = {}
    chunks = [(z, first, size) for z, size in enumerate((7, 6, 5, 4)) for first in range(0, 3 * size, size)]
    waited = set()
    build = iter(())
    for n in range(len(chunks) + 1):
        if n < len(chunks):
            z, first, size = chunks[n]
            if first == 0 and z + 1 < STEPS:
                build = spread_taps(taps_all.at[z + 1], taps_pad, pick, matrices[(z + 1) % 2])
            convolve_chunk(z, first, size, n % 2)
            for _ in range(4):
                next(build, None)
        if n > 0:
            z, first, size = chunks[n - 1]
            if first // size < len(PIECES[z]):
                wait_slow(z, first // size)
            for k in range(size):
                finish_tile(z, first + k, k, (n - 1) % 2)
            done = 3 - (2 * size - first) // size - 1
            if done >= 3 - len(IMAGE_PIECES[z]):
                send_image(z, done - 3 + len(IMAGE_PIECES[z]))

    def wait_image(z, n):
        for k in range(STEPS):
            @pl.when((lat != freq_at) | (k != freq_at))
            def _():
                outgoing(z, k, n).wait_recv()

    for n in range(3):
        last = [high for _, high in IMAGE_PIECES[STEPS - 1]]
        if n + 3 - len(last) >= 0 and 96 * n in [low for low, _ in IMAGE_PIECES[STEPS - 1]]:
            @pl.when(me == STEPS - 1)
            def _():
                wait_image(STEPS - 1, [low for low, _ in IMAGE_PIECES[STEPS - 1]].index(96 * n))

        if n == 0:
            @pl.when(me != STEPS - 1)
            def _():
                wait_image(0, 0)

        for t in range(4 * n, 4 * n + 4, 2):
            total = slots[0, 24 * t : 24 * t + 48].astype(jnp.float32)
            for k in range(1, STEPS):
                total = total + slots[k, 24 * t : 24 * t + 48].astype(jnp.float32)
            total = total * factor
            for k in range(2):
                for g in range(3):
                    turned = turn_back(total[24 * k + 8 * g : 24 * k + 8 * g + 8])
                    out_ref[0, 8 * (t + k) : 8 * (t + k) + 8, 128 * (2 - g) : 128 * (3 - g)] = turned

    for z in range(STEPS):
        @pl.when((lat != freq_at) | (z != me))
        def _():
            for n in range(len(IMAGE_PIECES[z])):
                outgoing(z, freq_at, n).wait_send()

        @pl.when(me == z)
        def _():
            for copies in slow_copies(z):
                for copy in copies[1:]:
                    copy.wait_send()


def march(freq, surface, slow, taps, factor):
    tile = [pltpu.VMEM((WINDOW, 48, lanes), jnp.bfloat16) for lanes in (256, 256, 128)]
    peers = STEPS - 1
    return pl.pallas_call(
        functools.partial(march_kernel, factor),
        out_shape=jax.ShapeDtypeStruct((1, ROWS, CELLS), jnp.float32),
        in_specs=[pl.BlockSpec(memory_space=pltpu.SMEM)] + [pl.BlockSpec(memory_space=pl.ANY)] * 3,
        out_specs=pl.BlockSpec(memory_space=pltpu.VMEM),
        scratch_shapes=tile + tile + [
            pltpu.VMEM((2560, 256), jnp.bfloat16),
            pltpu.VMEM((2560, 256), jnp.bfloat16),
            pltpu.VMEM((336, 256), jnp.float32),
            pltpu.VMEM((336, 256), jnp.float32),
            pltpu.VMEM((2, 2, ROWS + 4 * REACH * STEPS, CELLS), jnp.bfloat16),
            pltpu.VMEM((CELLS, CELLS), jnp.float32),
            pltpu.VMEM((CELLS + 2 * REACH * STEPS, CELLS), jnp.int16),
            pltpu.VMEM((STEPS, ROWS + 2 * REACH * STEPS, CELLS), jnp.int16),
            pltpu.VMEM((STEPS, 25, 2, 25), jnp.bfloat16),
            pltpu.VMEM((64, 128), jnp.float32),
            pltpu.VMEM((128, 256), jnp.bfloat16),
            pltpu.VMEM((STEPS, 288, 128), jnp.bfloat16),
            pltpu.VMEM((STEPS, 288, 128), jnp.bfloat16),
            pltpu.SemaphoreType.DMA((6,)),
            pltpu.SemaphoreType.DMA((1,)),
            pltpu.SemaphoreType.DMA((peers,)),
            pltpu.SemaphoreType.DMA((peers,)),
            pltpu.SemaphoreType.DMA((3, STEPS)),
            pltpu.SemaphoreType.DMA((STEPS, 3)),
            pltpu.SemaphoreType.DMA((STEPS, 3)),
            pltpu.SemaphoreType.DMA((STEPS, 3)),
        ],
        compiler_params=pltpu.CompilerParams(collective_id=0, has_side_effects=True, vmem_limit_bytes=48 << 20),
    )(freq, *(pltpu.with_memory_space_constraint(x, pltpu.HBM) for x in (surface, slow, taps)))


def on_device_fused(surface, kernels, slowness, freq_index):
    fixed = (2, 1, 2, CELLS, CELLS) == surface.shape and kernels.shape == (1, 1, 2, 25, 25)
    if not fixed:
        return on_device_general(surface, kernels, slowness, freq_index)
    factor = 1.0 / math.sqrt(lax.axis_size("freq"))
    return march(freq_index, surface, slowness, jnp.swapaxes(kernels, 2, 3), factor)


def fits(mesh):
    return mesh.shape["depth"] == 4 and mesh.shape["freq"] == 4


def solution(mesh):
    in_specs = (
        P("shots", "freq", None, None, None),
        P("depth", "freq", None, None, None),
        P("depth", None, None),
        P("freq"),
    )
    out_specs = P(("shots", "depth"), "freq", None)
    body = on_device_fused if fits(mesh) else on_device_general
    return jax.shard_map(
        body, mesh=mesh, in_specs=in_specs, out_specs=out_specs, check_vma=False
    )
```

```python
import functools
import math

import jax
import jax.numpy as jnp
from jax import lax
from jax.experimental import pallas as pl
from jax.experimental.pallas import tpu as pltpu
from jax.sharding import PartitionSpec as P


def with_halo(shard, sides, width):
    for axis, dim in sides:
        size, length = (lax.axis_size(axis), shard.shape[dim])
        up = [(i, (i + 1) % size) for i in range(size - 1)]
        down = [(j, i) for i, j in up]
        last = lax.slice_in_dim(shard, length - width, length, axis=dim)
        leading = lax.slice_in_dim(shard, 0, width, axis=dim)
        before = lax.ppermute(last, axis, up)
        after = lax.ppermute(leading, axis, down)
        shard = jnp.concatenate([before, shard, after], axis=dim)
    return shard


def convolve(padded, stencil, margin):
    rows_in = padded.shape[3]
    cells_y = padded.shape[4]
    tap_count = stencil.shape[-1]
    rows_out = rows_in - 2 * margin
    real_part = stencil[:, 0].astype(jnp.float32)
    imag_part = stencil[:, 1].astype(jnp.float32)
    filters = jnp.stack(
        [jnp.stack([real_part, -imag_part], 1), jnp.stack([imag_part, real_part], 1)], 1
    )
    offsets = lax.iota(jnp.int32, rows_in)[None, :] - lax.iota(jnp.int32, rows_out)[:, None]
    select = (offsets[None] == lax.iota(jnp.int32, tap_count)[:, None, None]).astype(jnp.float32)
    banded = jnp.einsum("fdcab,axk->fdxbck", filters, select).astype(jnp.bfloat16)
    widened = jnp.pad(padded, ((0, 0), (0, 0), (0, 0), (0, 0), (margin, margin)))
    patches = jnp.stack(
        [widened[:, :, :, :, shift : shift + cells_y] for shift in range(tap_count)], 0
    )
    return jnp.einsum("bwfcky,fdxbck->wfdxy", patches, banded, preferred_element_type=jnp.float32)


def rotate(convolved, phase_rate, freq_bins):
    phases = freq_bins[:, None, None] * phase_rate[None]
    cosines = jnp.cos(phases)
    sine_terms = jnp.sin(phases)
    real_out = convolved[:, :, 0] * cosines - convolved[:, :, 1] * sine_terms
    imag_out = convolved[:, :, 0] * sine_terms + convolved[:, :, 1] * cosines
    return jnp.stack([real_out, imag_out], 2).astype(jnp.bfloat16)


def correlate(stepped):
    widened = stepped.astype(jnp.float32)
    return jnp.sum(
        widened[0, :, 0] * widened[1, :, 0] + widened[0, :, 1] * widened[1, :, 1], axis=0
    )


def on_device_general(surface, kernels, slowness, freq_index):
    depth_count = lax.axis_size("depth")
    position = lax.axis_index("depth")
    cells_x = surface.shape[3]
    row_count = cells_x // depth_count
    tap_count = kernels.shape[-1]
    margin = (tap_count - 1) // 2
    start_row = position * row_count
    wavefield = lax.dynamic_slice_in_dim(surface, start_row, row_count, 3)
    stencils = lax.all_gather(kernels, "depth", axis=0, tiled=True)
    phase_rates = lax.all_to_all(slowness, "depth", split_axis=1, concat_axis=0, tiled=True)
    freq_bins = freq_index.astype(jnp.float32)

    def advance(wave, operands):
        stencil, phase_rate = operands
        padded = with_halo(wave, (("depth", 3),), margin)
        stepped = rotate(convolve(padded, stencil, margin), phase_rate, freq_bins)
        return (stepped, correlate(stepped))

    final_wave, partials = lax.scan(advance, wavefield, (stencils, phase_rates))
    moved = lax.all_to_all(partials, "depth", split_axis=0, concat_axis=1, tiled=True)
    summed = lax.psum_scatter(moved, "freq", scatter_dimension=1, tiled=True)
    return summed * (1.0 / math.sqrt(surface.shape[1] * lax.axis_size("freq")))


MESH = pl.DeviceIdType.MESH
SCALE = 32767.0 / 0.02
TX, TY, REACH, STEPS, ROWS, CELLS = 8, 16, 12, 4, 96, 384
PLANE_TILES = CELLS // TX
PIECES = (((16, 192),), ((32, 176),), ((32, 176),), ((48, 160),))
IMAGE_PIECES = (((0, 288),),) * 3 + (((0, 192), (192, 288)),)
LEAD = REACH * STEPS + 8
WINDOW = (ROWS + 2 * REACH * STEPS) // TX
SINE = (1.414213201146787, -0.23570044870069473, 0.011782564917166203, -0.00027913063632810375, 3.524705887741897e-06)
COSINE = (1.4142128454174687, -0.7070977888086795, 0.0589074886457319, -0.0019514243489185956, 3.136662365288423e-05)


def iotas(rows):
    return (lax.broadcasted_iota(jnp.int32, (rows, 128), 0), lax.broadcasted_iota(jnp.int32, (rows, 128), 1))


def turn(block):
    group = iotas(8)[1] >> 4
    block = pltpu.roll(block, 16, 1, stride=16, stride_axis=0)
    for k in range(3):
        block = jnp.where((group >> k) & 1 == 1, pltpu.roll(block, 8 - (1 << k), 0), block)
    return pltpu.roll(block, 0, 1, stride=16, stride_axis=0)


def turn_back(block):
    return turn(turn(turn(block)))


def rotor(phase_half):
    sq = phase_half * phase_half
    sine = jnp.full_like(sq, SINE[-1])
    for value in SINE[-2::-1]:
        sine = sine * sq + value
    sine = sine * phase_half
    cosine = jnp.full_like(sq, COSINE[-1])
    for value in COSINE[-2::-1]:
        cosine = cosine * sq + value
    return sine * cosine, 1.0 - sine * sine


def emit(wave, at, values):
    plain, beside, ends = wave
    sub, lane = iotas(8)
    dy = lane & 15
    low = dy < 8
    middle = (dy >= 4) & (dy < 12)
    sides, rests = [], []
    for w in range(2):
        side, rest = [], []
        for c in range(2):
            v = values[w][c]
            down = [pltpu.roll(x, 1, 0) for x in v]
            up = [pltpu.roll(x, 7, 0) for x in v]
            after = [jnp.where(sub == 0, down[g - 1] if g else 0.0, down[g]) for g in range(3)]
            before = [jnp.where(sub == 7, up[g + 1] if g < 2 else 0.0, up[g]) for g in range(3)]
            side.append([jnp.where(low, a, b) for a, b in zip(after, before)])
            rest.append([jnp.where(low, b, a) for a, b in zip(after, before)])
        sides.append(side)
        rests.append([jnp.where(middle, a, pltpu.roll(b, 8, 1)) for a, b in zip(*rest)])
    for c in range(2):
        across = slice(128 * c, 128 * c + 128)
        plain[at, :, across] = jnp.concatenate(values[0][c] + values[1][c], 0).astype(jnp.bfloat16)
        beside[at, :, across] = jnp.concatenate(sides[0][c] + sides[1][c], 0).astype(jnp.bfloat16)
    ends[at] = jnp.concatenate(rests[0] + rests[1], 0).astype(jnp.bfloat16)


def spread_taps(taps_ref, padded, pick, matrix):
    sub, lane = iotas(16)
    diag = (lane & 15) >= sub
    first = iotas(8)[0] < 4
    zero = jnp.zeros((16, 128), jnp.float32)
    for a in range(25):
        padded[2 * a : 2 * a + 2, 0:25] = taps_ref[a].astype(jnp.float32)
    spread = jnp.dot(padded[...].astype(jnp.bfloat16), pick[...], preferred_element_type=jnp.float32)
    lines = {}
    for p in range(2):
        chosen = ((sub & 1) == p) & (7 - (sub >> 1) == lane >> 4)
        for e in range(2):
            for v in range(4):
                part = spread[16 * (3 - v) : 16 * (3 - v) + 16, 128 * e : 128 * e + 128]
                line = jnp.sum(jnp.where(chosen, part, 0.0), axis=0, keepdims=True)
                lines[p, e, v] = jnp.broadcast_to(line, (16, 128))
    yield

    def windows(shift):
        found = []
        keep = lane >= sub + 16 * shift
        for p in range(2):
            pair = []
            for e in range(2):
                turned = [zero]
                for v in range(4):
                    turned.append(pltpu.roll(lines[p, e, v], 16 * shift, 1, stride=1, stride_axis=0))
                turned.append(zero)
                pair.append([jnp.where(keep, turned[v + 1], turned[v]) for v in range(5)])
            found.append(pair)
        return found

    start = windows(0)
    here = start
    last = [[jnp.where(diag, start[p][1][3 - di], 0.0) for p in range(2)] for di in range(4)]
    for dx in range(8):
        there = windows(dx + 1) if dx < 7 else start
        for di in range(4):
            v = 4 - di
            u = v if dx < 7 else v - 1
            mid, plus, minus = [], [], []
            for p in range(2):
                mid.append(jnp.where(diag, there[p][0][u], here[p][1][v]))
                plus.append(jnp.where(diag, there[p][1][u], 0.0))
                minus.append(jnp.where(diag, 0.0, here[p][0][v]))
            side = [jnp.concatenate([a[:8], b[8:]], 0) for a, b in zip(plus, minus)]
            for k, (real, imag) in enumerate((mid, side)):
                at = 640 * di + 256 * k + 16 * dx
                real, imag, back = real.astype(jnp.bfloat16), imag.astype(jnp.bfloat16), (-imag).astype(jnp.bfloat16)
                matrix[at : at + 16, 0:128] = real
                matrix[at : at + 16, 128:256] = imag
                matrix[at + 128 : at + 144, 0:128] = back
                matrix[at + 128 : at + 144, 128:256] = real
            at = 640 * di + 512 + 16 * dx
            for k in range(2):
                mine = (minus[k][:8], plus[k][8:])
                crossed = (-last[di][1][8:], -minus[1][:8]) if k == 0 else (last[di][0][8:], minus[0][:8])
                rows = [jnp.where(first, crossed[0], mine[0]), jnp.where(first, mine[1], crossed[1])]
                matrix[at : at + 16, 128 * k : 128 * k + 128] = jnp.concatenate(rows, 0).astype(jnp.bfloat16)
            last[di] = plus
        here = there
        yield


def swap(position):
    return 2 * (position % 2) + position // 2


def lateral(depth, freq):
    return swap(lax.rem(depth + 2 * freq, STEPS))


def march_kernel(factor, freq_ref, surface_ref, slow_ref, taps_ref, out_ref,
                 plain0, beside0, ends0, plain1, beside1, ends1, matrix0, matrix1, sums0, sums1,
                 field, slow_raw, slow_own, slow_all, taps_all, taps_pad, pick, image, slots,
                 loaded, send, recv, slow_send, slow_recv, image_send, image_recv):
    me = lax.axis_index("depth")
    freq_at = lax.axis_index("freq")
    lat = lateral(me, freq_at)
    waves = ((plain0, beside0, ends0), (plain1, beside1, ends1))
    matrices = (matrix0, matrix1)
    sums = (sums0, sums1)
    margin = REACH * STEPS
    sub, lane = iotas(8)

    slow_load = pltpu.make_async_copy(slow_ref.at[0], slow_raw, loaded.at[1])
    slow_load.start()

    barrier = pltpu.get_barrier_semaphore()
    for step in range(1, STEPS):
        pl.semaphore_signal(barrier, inc=1, device_id={"depth": lax.rem(me + step, STEPS)}, device_id_type=MESH)
    for k in range(STEPS):
        @pl.when((lat != freq_at) | (k != freq_at))
        def _():
            source = lax.rem(swap(freq_at) + 2 * k, STEPS)
            pl.semaphore_signal(barrier, inc=1, device_id={"depth": source, "freq": k}, device_id_type=MESH)

    blank = jnp.zeros((margin, CELLS), field.dtype)
    for w in range(2):
        for c in range(2):
            field[w, c, margin : 2 * margin] = blank
            field[w, c, ROWS + 2 * margin : ROWS + 3 * margin] = blank
    start = pl.multiple_of(jnp.clip(lat * ROWS - margin, 0, CELLS - ROWS - 2 * margin), 16)
    offset = pl.multiple_of(start - lat * ROWS + 2 * margin, 16)
    surface_loads = [
        pltpu.make_async_copy(
            surface_ref.at[w, 0, c, pl.ds(start, ROWS + 2 * margin)],
            field.at[w, c, pl.ds(offset, ROWS + 2 * margin)], loaded.at[2 + 2 * w + c])
        for w in range(2) for c in range(2)
    ]
    for copy in surface_loads:
        copy.start()

    taps_pad[...] = jnp.zeros_like(taps_pad)
    row, column = lax.broadcasted_iota(jnp.int32, (128, 256), 0), lax.broadcasted_iota(jnp.int32, (128, 256), 1)
    pick[...] = jnp.where(row == jnp.where(column < 128, 12, 28) - (column & 15), 1.0, 0.0).astype(jnp.bfloat16)

    taps_copies = [
        pltpu.make_async_remote_copy(
            src_ref=taps_ref.at[0, 0], dst_ref=taps_all.at[me], send_sem=send.at[step - 1], recv_sem=recv.at[me],
            device_id={"depth": lax.rem(me + step, STEPS)}, device_id_type=MESH)
        for step in range(1, STEPS)
    ] + [pltpu.make_async_copy(taps_ref.at[0, 0], taps_all.at[me], recv.at[me])]

    def enter():
        pl.semaphore_wait(barrier, 2 * STEPS - 1 - (lat == freq_at).astype(jnp.int32))
        for copy in taps_copies:
            copy.start()

    @pl.when(me == 0)
    def _():
        enter()

    slow_load.wait()
    for at in range(0, slow_own.shape[0], 16):
        halves = [
            jnp.round(slow_raw[low : low + 8] * SCALE) if 0 <= low < CELLS else jnp.zeros((8, CELLS), jnp.float32)
            for low in (at - LEAD, at - LEAD + 8)
        ]
        slow_own[at : at + 16] = jnp.concatenate(halves, 0).astype(jnp.int32).astype(jnp.int16)

    def slow_copies(z):
        pieces = []
        for n, (low, high) in enumerate(PIECES[z]):
            copies = []
            for step in range(STEPS):
                other = lax.rem(z + step, STEPS)
                at = pl.multiple_of(lateral(other, freq_at) * ROWS + low, 16)
                source = slow_own.at[pl.ds(at, high - low)]
                target = slow_all.at[z, low:high]
                if step:
                    copies.append(pltpu.make_async_remote_copy(
                        src_ref=source, dst_ref=target, send_sem=slow_send.at[n, step], recv_sem=slow_recv.at[z, n],
                        device_id={"depth": other}, device_id_type=MESH))
                else:
                    copies.append(pltpu.make_async_copy(source, target, slow_recv.at[z, n]))
            pieces.append(copies)
        return pieces

    def start_slow(z):
        @pl.when(me == z)
        def _():
            for copies in slow_copies(z):
                for copy in copies:
                    copy.start()

    def wait_slow(z, n):
        slow_copies(z)[n][0].wait()

    @pl.when(me != 0)
    def _():
        enter()

    for z in range(0, STEPS, 2):
        start_slow(z)

    for copy in surface_loads:
        copy.wait()

    for pair in range(WINDOW // 2):
        rows = slice(margin + 16 * pair, margin + 16 * pair + 16)
        both = [field[w, c, rows, :].astype(jnp.float32) for w in range(2) for c in range(2)]
        for k in range(2):
            tiles = [turn(x[8 * k : 8 * k + 8, 128 * g : 128 * g + 128]) for x in both for g in (2, 1, 0)]
            emit(waves[0], 2 * pair + k, [[tiles[6 * w + 3 * c : 6 * w + 3 * c + 3] for c in range(2)] for w in range(2)])

    def wait_taps(z):
        pltpu.make_async_copy(taps_ref.at[0, 0], taps_all.at[z], recv.at[z]).wait()

    start_slow(1)
    wait_taps(0)
    for _ in spread_taps(taps_all.at[0], taps_pad, pick, matrices[0]):
        pass
    start_slow(3)
    for z in range(1, STEPS):
        wait_taps(z)

    freq = freq_ref[0].astype(jnp.float32) * (0.5 / SCALE)

    def outgoing(z, k, n):
        low, high = IMAGE_PIECES[z][n]
        return pltpu.make_async_remote_copy(
            src_ref=image.at[z, low:high], dst_ref=slots.at[k, low:high],
            send_sem=image_send.at[z, n], recv_sem=image_recv.at[k, n],
            device_id={"depth": z, "freq": lat}, device_id_type=MESH)

    def send_image(z, n):
        low, high = IMAGE_PIECES[z][n]
        own = (lat == freq_at) & (z == me)

        @pl.when(jnp.logical_not(own))
        def _():
            outgoing(z, freq_at, n).start()

        @pl.when(own)
        def _():
            slots[freq_at, low:high] = image[z, low:high]

    def convolve_chunk(z, first, size, slot):
        pieces = []
        for di in range(4):
            for ref in waves[z % 2]:
                pieces.append(ref[first + di : first + di + size].reshape(48 * size, ref.shape[2]))
        sums[slot][: 48 * size] = jnp.dot(
            jnp.concatenate(pieces, 1), matrices[z % 2][...], preferred_element_type=jnp.float32)

    products, coded_rows = {}, {}

    def slow_rows(z, n):
        if (z, n // 2) not in coded_rows:
            coded_rows[z, n // 2] = slow_all[z, 16 * (n // 2) : 16 * (n // 2) + 16].astype(jnp.int32).astype(jnp.float32)
            coded_rows.pop((z, n // 2 - 2), None)
        return [coded_rows[z, n // 2][8 * (n % 2) : 8 * (n % 2) + 8, 128 * g : 128 * g + 128] for g in range(3)]

    def finish_tile(z, i, at, slot):
        halo = REACH * (STEPS - 1 - z)
        low = LEAD - REACH * (STEPS - 1 - z) + 8 * i
        parts = slow_rows(z, low // 8)
        if low % 8:
            parts = [pltpu.roll(jnp.where(sub < 4, b, a), 4, 0) for a, b in zip(parts, slow_rows(z, low // 8 + 1))]
        sine, cosine = rotor(jnp.concatenate([turn(parts[g]) for g in (2, 1, 0)], 0) * freq)
        if 8 * i < halo or 8 * i + 8 > ROWS + halo:
            x = (lane >> 4) + (lat * ROWS - halo + 8 * i)
            inside = (x >= 0) & (x < CELLS)
        else:
            inside = None
        values = [[[], []], [[], []]]
        for g in range(3):
            s, c = sine[8 * g : 8 * g + 8], cosine[8 * g : 8 * g + 8]
            if inside is not None:
                s, c = jnp.where(inside, s, 0.0), jnp.where(inside, c, 0.0)
            for w in range(2):
                rows = slice(48 * at + 24 * w + 8 * g, 48 * at + 24 * w + 8 * g + 8)
                real, imag = sums[slot][rows, 0:128], sums[slot][rows, 128:256]
                for k, value in enumerate((real * c - imag * s, real * s + imag * c)):
                    values[w][k].append(value.astype(jnp.bfloat16).astype(jnp.float32))
        if z + 1 < STEPS:
            emit(waves[(z + 1) % 2], i, values)
        if 8 * i + 8 > halo and 8 * i < ROWS + halo:
            (a, b), (c, d) = values
            products[z, i] = [a[g] * c[g] + b[g] * d[g] for g in range(3)]
        whole = halo % 8 == 0
        t = i - halo // 8 if whole else i - halo // 8 - 1
        if 0 <= t < ROWS // 8:
            here = products[z, i]
            if not whole:
                here = [pltpu.roll(jnp.where(lane < 64, b, a), 64, 1) for a, b in zip(products[z, i - 1], here)]
            held_image[t] = here
            if t % 2 == 1:
                image[z, 24 * (t - 1) : 24 * (t + 1)] = jnp.concatenate(held_image.pop(t - 1) + held_image.pop(t), 0).astype(image.dtype)

    held_image = {}
    chunks = [(z, first, size) for z, size in enumerate((7, 6, 5, 4)) for first in range(0, 3 * size, size)]
    waited = set()
    build = iter(())
    for n in range(len(chunks) + 1):
        if n < len(chunks):
            z, first, size = chunks[n]
            if first == 0 and z + 1 < STEPS:
                build = spread_taps(taps_all.at[z + 1], taps_pad, pick, matrices[(z + 1) % 2])
            convolve_chunk(z, first, size, n % 2)
            for _ in range(4):
                next(build, None)
        if n > 0:
            z, first, size = chunks[n - 1]
            if first // size < len(PIECES[z]):
                wait_slow(z, first // size)
            for k in range(size):
                finish_tile(z, first + k, k, (n - 1) % 2)
            done = 3 - (2 * size - first) // size - 1
            if done >= 3 - len(IMAGE_PIECES[z]):
                send_image(z, done - 3 + len(IMAGE_PIECES[z]))

    def wait_image(z, n):
        for k in range(STEPS):
            @pl.when((lat != freq_at) | (k != freq_at))
            def _():
                outgoing(z, k, n).wait_recv()

    for n in range(3):
        last = [high for _, high in IMAGE_PIECES[STEPS - 1]]
        if n + 3 - len(last) >= 0 and 96 * n in [low for low, _ in IMAGE_PIECES[STEPS - 1]]:
            @pl.when(me == STEPS - 1)
            def _():
                wait_image(STEPS - 1, [low for low, _ in IMAGE_PIECES[STEPS - 1]].index(96 * n))

        if n == 0:
            @pl.when(me != STEPS - 1)
            def _():
                wait_image(0, 0)

        for t in range(4 * n, 4 * n + 4, 2):
            total = slots[0, 24 * t : 24 * t + 48].astype(jnp.float32)
            for k in range(1, STEPS):
                total = total + slots[k, 24 * t : 24 * t + 48].astype(jnp.float32)
            total = total * factor
            for k in range(2):
                for g in range(3):
                    turned = turn_back(total[24 * k + 8 * g : 24 * k + 8 * g + 8])
                    out_ref[0, 8 * (t + k) : 8 * (t + k) + 8, 128 * (2 - g) : 128 * (3 - g)] = turned

    for copy in taps_copies[:-1]:
        copy.wait_send()
    for z in range(STEPS):
        @pl.when((lat != freq_at) | (z != me))
        def _():
            for n in range(len(IMAGE_PIECES[z])):
                outgoing(z, freq_at, n).wait_send()

        @pl.when(me == z)
        def _():
            for copies in slow_copies(z):
                for copy in copies[1:]:
                    copy.wait_send()


def march(freq, surface, slow, taps, factor):
    tile = [pltpu.VMEM((WINDOW, 48, lanes), jnp.bfloat16) for lanes in (256, 256, 128)]
    peers = STEPS - 1
    return pl.pallas_call(
        functools.partial(march_kernel, factor),
        out_shape=jax.ShapeDtypeStruct((1, ROWS, CELLS), jnp.float32),
        in_specs=[pl.BlockSpec(memory_space=pltpu.SMEM)] + [pl.BlockSpec(memory_space=pl.ANY)] * 3,
        out_specs=pl.BlockSpec(memory_space=pltpu.VMEM),
        scratch_shapes=tile + tile + [
            pltpu.VMEM((2560, 256), jnp.bfloat16),
            pltpu.VMEM((2560, 256), jnp.bfloat16),
            pltpu.VMEM((336, 256), jnp.float32),
            pltpu.VMEM((336, 256), jnp.float32),
            pltpu.VMEM((2, 2, ROWS + 4 * REACH * STEPS, CELLS), jnp.bfloat16),
            pltpu.VMEM((CELLS, CELLS), jnp.float32),
            pltpu.VMEM((CELLS + 2 * REACH * STEPS, CELLS), jnp.int16),
            pltpu.VMEM((STEPS, ROWS + 2 * REACH * STEPS, CELLS), jnp.int16),
            pltpu.VMEM((STEPS, 25, 2, 25), jnp.bfloat16),
            pltpu.VMEM((64, 128), jnp.float32),
            pltpu.VMEM((128, 256), jnp.bfloat16),
            pltpu.VMEM((STEPS, 288, 128), jnp.bfloat16),
            pltpu.VMEM((STEPS, 288, 128), jnp.bfloat16),
            pltpu.SemaphoreType.DMA((6,)),
            pltpu.SemaphoreType.DMA((peers,)),
            pltpu.SemaphoreType.DMA((STEPS,)),
            pltpu.SemaphoreType.DMA((3, STEPS)),
            pltpu.SemaphoreType.DMA((STEPS, 3)),
            pltpu.SemaphoreType.DMA((STEPS, 3)),
            pltpu.SemaphoreType.DMA((STEPS, 3)),
        ],
        compiler_params=pltpu.CompilerParams(collective_id=0, has_side_effects=True, vmem_limit_bytes=48 << 20),
    )(freq, *(pltpu.with_memory_space_constraint(x, pltpu.HBM) for x in (surface, slow, taps)))


def on_device_fused(surface, kernels, slowness, freq_index):
    fixed = (2, 1, 2, CELLS, CELLS) == surface.shape and kernels.shape == (1, 1, 2, 25, 25)
    if not fixed:
        return on_device_general(surface, kernels, slowness, freq_index)
    factor = 1.0 / math.sqrt(lax.axis_size("freq"))
    return march(freq_index, surface, slowness, jnp.swapaxes(kernels, 2, 3), factor)


def fits(mesh):
    return mesh.shape["depth"] == 4 and mesh.shape["freq"] == 4


def solution(mesh):
    in_specs = (
        P("shots", "freq", None, None, None),
        P("depth", "freq", None, None, None),
        P("depth", None, None),
        P("freq"),
    )
    out_specs = P(("shots", "depth"), "freq", None)
    body = on_device_fused if fits(mesh) else on_device_general
    return jax.shard_map(
        body, mesh=mesh, in_specs=in_specs, out_specs=out_specs, check_vma=False
    )
```
